32 devices in a mesh: case: 2 (over y), mode: 4 (over z), harm: 2 (over x), rad: 2 (over core).
Axes of the slice: x: 2, y: 2, z: 4, core: 2. Of those that a mesh axis runs over, the one named last changes fastest.
Arguments:
- direct_field: bfloat16 [16, 16, 2, 5, 16, 256], P(('case', 'harm'), 'mode', None, None, None, 'rad'), parts along dimension 0, may hold values from -6 to 6
- adjoint_field: bfloat16 [16, 16, 2, 5, 16, 256], P(('case', 'harm'), 'mode', None, None, None, 'rad'), parts along dimension 0, may hold values from -6 to 6
- triad_slots: int32 [16, 4, 2], P('mode'), may hold values from 0 to 3
Outputs:
- sensitivity: float32 [32, 2, 5, 16, 256], P(('case', 'harm'), None, None, 'mode', 'rad'), parts along dimension 0
The draws below stay inside these ranges and needn't reach their ends.
There are 2 independent parts, one for each index of `case`. The reference program is written for one: setup_inputs(seed, part) draws one part's arguments, and reference() takes and returns one part's arrays. A program takes and returns all parts, laid end to end along the dimension named above; an argument that names none is the same for every part. Nothing has to cross between parts.
Inputs may be any that keep to these rules, and one draw needn't show every extreme that they name: triad_slots[m, s, 0] is the slot, within the block of 4 modes holding m, of the adjoint factor; triad_slots[m, s, 1] is the slot of the direct factor within the block s blocks below m's block, counted cyclically over 4 blocks.
All inputs are finite; a program needn't handle non-finite values.
Results may differ from the reference program's by a relative error of at most 0.0003.
Values may be sent and summed in bfloat16 or wider, within the bound.
A program may use at most 64 MiB of HBM per device.

```python
import math
import jax
import jax.numpy as jnp
from jax import lax

FIELDS = 5
HARMS = 8
MODE_DEV = 4
NX = 16
MODES = 16
STOPS = 4
RADIAL = 256


def with_ends(result, stream_key, least, high):
    longest = result.shape.index(max(result.shape))
    spots = []
    for shift in (0, 1):
        where = [jax.random.randint(jax.random.fold_in(stream_key, axis), (), 0, length) for axis, length in enumerate(result.shape)]
        where[longest] = (where[longest] + shift) % result.shape[longest]
        spots.append(tuple(where))
    return result.at[spots[0]].set(least).at[spots[1]].set(high)


def steps_of(rng, extent, pieces, least, high):
    factor_of, own = 1.0, jax.random.fold_in(rng, 6)
    for dim, parts in pieces:
        heights = jnp.exp(jax.random.uniform(jax.random.fold_in(own, dim), (parts,), jnp.float32, least / len(pieces), high / len(pieces)))
        factor_of = factor_of * jnp.repeat(heights, extent[dim] // parts).reshape([-1 if axis == dim else 1 for axis in range(len(extent))])
    return factor_of


def centred(stream_key, dims, width, reach, pieces=(), kind=jnp.bfloat16):
    level = steps_of(stream_key, dims, pieces, -0.22, 0.18) if pieces else 1.0
    result = jax.random.normal(stream_key, dims, jnp.float32) * width * level
    return jnp.minimum(jnp.maximum(result, -reach), reach).astype(kind)


def setup_inputs(seed: int = 0, part: int = 0) -> dict:
    seeds = jax.random.split(jax.random.key(seed), 4)
    part_keys = jax.random.split(jax.random.fold_in(seeds[3], part), 4)
    return {
        "direct_field": centred(part_keys[0], (HARMS, MODES, 2, FIELDS, NX, RADIAL), 1.0, 6.0, ((0, 2), (1, 4), (5, 2))),
        "adjoint_field": centred(part_keys[1], (HARMS, MODES, 2, FIELDS, NX, RADIAL), 1.0, 6.0, ((0, 2), (1, 4), (5, 2))),
        "triad_slots": with_ends(jax.random.randint(seeds[2], (MODES, STOPS, 2), 0, MODE_DEV), jax.random.fold_in(seeds[2], 1), 0, MODE_DEV - 1).astype(jnp.int32),
    }


def stencil(padded, axis, length):

    def shifted(offset):
        return lax.slice_in_dim(padded, offset, offset + length, axis=axis)
    return (shifted(0) - 8.0 * shifted(1) + 8.0 * shifted(3) - shifted(4)) / 12.0

def derivative(source, axis):
    length = source.shape[axis]
    widths = [(0, 0)] * source.ndim
    widths[axis] = (2, 2)
    return stencil(jnp.pad(source, widths), axis, length)

def conj_product(left_side, right_side):
    left_real = left_side[..., 0, :, :, :]
    left_imag = left_side[..., 1, :, :, :]
    right_real = right_side[..., 0, :, :, :]
    right_imag = right_side[..., 1, :, :, :]
    return jnp.stack([left_real * right_real + left_imag * right_imag, left_real * right_imag - left_imag * right_real], axis=-4)

def triad_term(adjoint, adjoint_axial, adjoint_radial, direct, direct_axial, direct_radial):
    total_sum = conj_product(direct[..., 1:2, :, :], adjoint_axial)
    total_sum = total_sum + conj_product(direct[..., 2:3, :, :], adjoint_radial)
    total_sum = total_sum + conj_product(direct_axial, adjoint[..., 1:2, :, :])
    return total_sum + conj_product(direct_radial, adjoint[..., 2:3, :, :])

def reference(direct_field, adjoint_field, triad_slots):
    direct = direct_field.astype(jnp.float32)
    direct_axial = derivative(direct, 4)
    direct_radial = derivative(direct, 5)
    adjoint = adjoint_field.astype(jnp.float32)
    adjoint_axial = derivative(adjoint, 4)
    adjoint_radial = derivative(adjoint, 5)
    scale = 1.0 / math.sqrt(8.0 * STOPS * HARMS)

    def select(source, position):
        return lax.dynamic_index_in_dim(source, position, axis=1, keepdims=False)

    def one_mode(mode_index):
        block_index = mode_index // MODE_DEV

        def one_stop(running, stop_index):
            slot_pair = triad_slots[mode_index, stop_index]
            adjoint_mode = block_index * MODE_DEV + slot_pair[0]
            direct_mode = (block_index - stop_index) % STOPS * MODE_DEV + slot_pair[1]
            term = triad_term(select(adjoint, adjoint_mode), select(adjoint_axial, adjoint_mode), select(adjoint_radial, adjoint_mode), select(direct, direct_mode), select(direct_axial, direct_mode), select(direct_radial, direct_mode))
            return (running + lax.optimization_barrier(jnp.sum(term, axis=0)), None)
        start_sum = jnp.zeros((2, FIELDS, NX, RADIAL), jnp.float32)
        running, _ = lax.scan(one_stop, start_sum, jnp.arange(STOPS, dtype=jnp.int32))
        return running * scale
    return lax.map(one_mode, jnp.arange(MODES, dtype=jnp.int32))
```

```python
import functools
import math

import jax
import jax.numpy as jnp
from jax import lax
from jax.experimental import pallas as pl
from jax.experimental.pallas import tpu as pltpu
from jax.sharding import PartitionSpec as P

HARMS = 8
SLOTS = 4
FIELDS = 5
PLANES = 2 * FIELDS
MESH = pl.DeviceIdType.MESH


def coefficient(offset):
    value = jnp.where(offset == 1, 8.0, 0.0)
    value = jnp.where(offset == -1, -8.0, value)
    value = jnp.where(offset == 2, -1.0, value)
    value = jnp.where(offset == -2, 1.0, value)
    return value


def kernel(
    n, hs, kh, nx,
    slots, d_ref, a_ref, out_ref,
    gbuf, pbuf, apbuf,
    d_st, dx_st, dr_st, a_st, ax_st, ar_st,
    run, sbuf, rbuf, radial, axial,
    right_send, right_recv, left_send, left_recv,
    core_send, core_recv, adj_sem, slab_send, slab_recv,
):
    me = lax.axis_index("mode")
    my_harm = lax.axis_index("harm")
    core = lax.axis_index("rad")
    per_owner = n // hs
    cells = nx // n
    rows = d_ref.shape[0]
    chunk = axial.shape[0]

    barrier = pltpu.get_barrier_semaphore()

    def greet(index, carry):
        q = index // hs
        h = index % hs

        @pl.when(jnp.logical_or(q != me, h != my_harm))
        def _():
            pl.semaphore_signal(barrier, inc=1, device_id={"mode": q, "harm": h}, device_id_type=MESH)

        return carry

    lax.fori_loop(0, n * hs, greet, 0)
    pl.semaphore_signal(barrier, inc=1, device_id={"rad": 1 - core}, device_id_type=MESH)
    pl.semaphore_wait(barrier, n * hs)

    def to_right(src, block, hop):
        return pltpu.make_async_remote_copy(
            src_ref=src, dst_ref=gbuf.at[block],
            send_sem=right_send.at[hop], recv_sem=right_recv.at[hop],
            device_id={"mode": me + 1}, device_id_type=MESH)

    def to_left(src, block, hop):
        return pltpu.make_async_remote_copy(
            src_ref=src, dst_ref=gbuf.at[block],
            send_sem=left_send.at[hop], recv_sem=left_recv.at[hop],
            device_id={"mode": me - 1}, device_id_type=MESH)

    def to_core(src, block):
        return pltpu.make_async_remote_copy(
            src_ref=src, dst_ref=pbuf.at[block],
            send_sem=core_send.at[block], recv_sem=core_recv.at[block],
            device_id={"rad": 1 - core}, device_id_type=MESH)

    adj_copy = pltpu.make_async_remote_copy(
        src_ref=a_ref, dst_ref=apbuf, send_sem=adj_sem.at[0], recv_sem=adj_sem.at[1],
        device_id={"rad": 1 - core}, device_id_type=MESH)

    @pl.when(me < n - 1)
    def _():
        to_right(d_ref, me, 0).start()

    @pl.when(me > 0)
    def _():
        to_left(d_ref, me, 0).start()

    adj_copy.start()
    to_core(d_ref, me).start()

    row = lax.broadcasted_iota(jnp.int32, (128, 128), 0)
    col = lax.broadcasted_iota(jnp.int32, (128, 128), 1)
    shift = (1 - 2 * core) * 128
    radial[0:128, :] = coefficient(row - col).astype(jnp.bfloat16)
    radial[128:256, :] = coefficient(row - col + shift).astype(jnp.bfloat16)
    row = lax.broadcasted_iota(jnp.int32, (chunk, chunk), 0)
    col = lax.broadcasted_iota(jnp.int32, (chunk, chunk), 1)
    same = (row // nx) == (col // nx)
    axial[...] = jnp.where(same, coefficient(col - row), 0.0).astype(jnp.bfloat16)
    run[...] = jnp.zeros_like(run)

    def prepare(own, partner, plain, along_x, along_r):
        def step(i, carry):
            at = pl.ds(pl.multiple_of(i * chunk, chunk), chunk)
            planes = pl.ds(i * (chunk // nx), chunk // nx)
            mine = own[at, :]
            both = jnp.concatenate([mine, partner[at, :]], axis=1)
            shape = (chunk // nx, nx, 128)
            plain[planes] = mine.astype(jnp.float32).reshape(shape)
            along_r[planes] = jnp.dot(
                both, radial[...], preferred_element_type=jnp.float32).reshape(shape)
            along_x[planes] = jnp.dot(
                axial[...], mine, preferred_element_type=jnp.float32).reshape(shape)
            return carry

        lax.fori_loop(0, rows // chunk, step, 0)

    def products(stop):
        def one_mode(m, carry):
            adj_slot = slots[m, stop, 0]
            dir_slot = slots[m, stop, 1]
            for half in range(nx // 8):
                part = pl.ds(half * 8, 8)
                real = [run[m * PLANES + f, part, :] for f in range(FIELDS)]
                imag = [run[m * PLANES + FIELDS + f, part, :] for f in range(FIELDS)]
                for k in range(kh):
                    da = (k * SLOTS + adj_slot) * PLANES
                    dd = (k * SLOTS + dir_slot) * PLANES
                    d1r = d_st[dd + 1, part, :]
                    d2r = d_st[dd + 2, part, :]
                    d1i = d_st[dd + FIELDS + 1, part, :]
                    d2i = d_st[dd + FIELDS + 2, part, :]
                    a1r = a_st[da + 1, part, :]
                    a2r = a_st[da + 2, part, :]
                    a1i = a_st[da + FIELDS + 1, part, :]
                    a2i = a_st[da + FIELDS + 2, part, :]
                    for f in range(FIELDS):
                        axr = ax_st[da + f, part, :]
                        axi = ax_st[da + FIELDS + f, part, :]
                        arr = ar_st[da + f, part, :]
                        ari = ar_st[da + FIELDS + f, part, :]
                        dxr = dx_st[dd + f, part, :]
                        dxi = dx_st[dd + FIELDS + f, part, :]
                        drr = dr_st[dd + f, part, :]
                        dri = dr_st[dd + FIELDS + f, part, :]
                        real[f] = real[f] + (
                            ((d1r * axr + d1i * axi) + (d2r * arr + d2i * ari))
                            + ((dxr * a1r + dxi * a1i) + (drr * a2r + dri * a2i)))
                        imag[f] = imag[f] + (
                            ((d1r * axi - d1i * axr) + (d2r * ari - d2i * arr))
                            + ((dxr * a1i - dxi * a1r) + (drr * a2i - dri * a2r)))
                for f in range(FIELDS):
                    run[m * PLANES + f, part, :] = real[f]
                    run[m * PLANES + FIELDS + f, part, :] = imag[f]
            return carry

        lax.fori_loop(0, SLOTS, one_mode, 0)

    def visit(block, stop):
        to_core(gbuf.at[block], block).wait_recv()
        prepare(gbuf.at[block], pbuf.at[block], d_st, dx_st, dr_st)
        products(stop)

    def hop_step(hop, carry):
        from_left = me - hop
        from_right = me + hop

        @pl.when(from_left >= 0)
        def _():
            to_right(gbuf.at[from_left], from_left, hop - 1).wait_recv()
            to_core(gbuf.at[from_left], from_left).start()

            @pl.when(me < n - 1)
            def _():
                to_right(gbuf.at[from_left], from_left, hop).start()

        @pl.when(from_right < n)
        def _():
            to_left(gbuf.at[from_right], from_right, hop - 1).wait_recv()
            to_core(gbuf.at[from_right], from_right).start()

            @pl.when(me > 0)
            def _():
                to_left(gbuf.at[from_right], from_right, hop).start()

        return carry

    def visit_hop(hop):
        @pl.when(me - hop >= 0)
        def _():
            visit(me - hop, hop)

        @pl.when(me + hop < n)
        def _():
            visit(me + hop, n - hop)

    adj_copy.wait_recv()
    prepare(a_ref, apbuf, a_st, ax_st, ar_st)
    to_core(d_ref, me).wait_recv()
    prepare(d_ref, pbuf.at[me], d_st, dx_st, dr_st)
    products(0)

    def steps(hop, carry):
        @pl.when(hop < n)
        def _():
            hop_step(hop, 0)

        @pl.when(hop > 1)
        def _():
            visit_hop(hop - 1)

        return carry

    lax.fori_loop(1, n + 1, steps, 0)

    scale = 1.0 / (12.0 * math.sqrt(8.0 * n * HARMS))
    for q in range(n):
        sbuf[q] = run[:, q * cells:(q + 1) * cells, :] * scale

    owner = me // per_owner
    place = me % per_owner

    def slab(q, h, i):
        return pltpu.make_async_remote_copy(
            src_ref=sbuf.at[q], dst_ref=rbuf.at[h * per_owner + i],
            send_sem=slab_send.at[q], recv_sem=slab_recv.at[h * per_owner + i],
            device_id={"mode": q, "harm": owner}, device_id_type=MESH)

    def each_target(act):
        def step(q, carry):
            @pl.when(jnp.logical_or(q != me, owner != my_harm))
            def _():
                act(slab(q, my_harm, place))

            return carry

        lax.fori_loop(0, n, step, 0)

    each_target(lambda copy: copy.start())

    @pl.when(owner == my_harm)
    def _():
        rbuf[my_harm * per_owner + place] = sbuf[me]

    def arrive(index, carry):
        h = index // per_owner
        i = index % per_owner
        mine = jnp.logical_and(h == my_harm, my_harm * per_owner + i == me)

        @pl.when(jnp.logical_not(mine))
        def _():
            slab(0, h, i).wait_recv()

        return carry

    lax.fori_loop(0, hs * per_owner, arrive, 0)
    for i in range(per_owner):
        total = rbuf[i]
        for h in range(1, hs):
            total = total + rbuf[h * per_owner + i]
        out_ref[i] = total

    each_target(lambda copy: copy.wait_send())
    adj_copy.wait_send()

    def drain(block, carry):
        to_core(d_ref, block).wait_send()
        return carry

    lax.fori_loop(0, n, drain, 0)

    def drain_hops(hop, carry):
        @pl.when(jnp.logical_and(me - hop >= 0, me < n - 1))
        def _():
            to_right(d_ref, me, hop).wait_send()

        @pl.when(jnp.logical_and(me + hop < n, me > 0))
        def _():
            to_left(d_ref, me, hop).wait_send()

        return carry

    lax.fori_loop(0, n, drain_hops, 0)


def body(hs, direct_field, adjoint_field, triad_slots):
    n = triad_slots.shape[1]
    kh = direct_field.shape[0]
    nx = direct_field.shape[4]
    planes = kh * SLOTS * PLANES
    rows = planes * nx
    chunk = 256 if rows % 256 == 0 else 128
    cells = nx // n
    per_owner = n // hs
    f32, bf16 = jnp.float32, jnp.bfloat16
    dma = pltpu.SemaphoreType.DMA
    out = pl.pallas_call(
        functools.partial(kernel, n, hs, kh, nx),
        out_shape=jax.ShapeDtypeStruct((per_owner, SLOTS * PLANES, cells, 128), f32),
        in_specs=[pl.BlockSpec(memory_space=pltpu.SMEM)] + [pl.BlockSpec(memory_space=pltpu.VMEM)] * 2,
        out_specs=pl.BlockSpec(memory_space=pltpu.VMEM),
        scratch_shapes=[
            pltpu.VMEM((n, rows, 128), bf16),
            pltpu.VMEM((n, rows, 128), bf16),
            pltpu.VMEM((rows, 128), bf16),
        ] + [pltpu.VMEM((planes, nx, 128), f32)] * 6 + [
            pltpu.VMEM((SLOTS * PLANES, nx, 128), f32),
            pltpu.VMEM((n, SLOTS * PLANES, cells, 128), f32),
            pltpu.VMEM((hs * per_owner, SLOTS * PLANES, cells, 128), f32),
            pltpu.VMEM((256, 128), bf16),
            pltpu.VMEM((chunk, chunk), bf16),
            dma((n,)), dma((n,)), dma((n,)), dma((n,)),
            dma((n,)), dma((n,)), dma((2,)), dma((n,)), dma((hs * per_owner,)),
        ],
        compiler_params=pltpu.CompilerParams(
            collective_id=0, has_side_effects=True, vmem_limit_bytes=50 << 20),
    )(
        triad_slots,
        direct_field.reshape(rows, 128),
        adjoint_field.reshape(rows, 128),
    )
    return out.reshape(per_owner * SLOTS, 2, FIELDS, cells, 128)


def solution(mesh):
    return jax.shard_map(
        functools.partial(body, mesh.shape["harm"]),
        mesh=mesh,
        in_specs=(
            P(("case", "harm"), "mode", None, None, None, "rad"),
            P(("case", "harm"), "mode", None, None, None, "rad"),
            P("mode", None, None),
        ),
        out_specs=P(("case", "harm"), None, None, "mode", "rad"),
        check_vma=False,
    )
```

```python
import functools
import math

import jax
import jax.numpy as jnp
from jax import lax
from jax.experimental import pallas as pl
from jax.experimental.pallas import tpu as pltpu
from jax.sharding import PartitionSpec as P

HARMS = 8
SLOTS = 4
FIELDS = 5
PLANES = 2 * FIELDS
MESH = pl.DeviceIdType.MESH


def coefficient(offset):
    value = jnp.where(offset == 1, 8.0, 0.0)
    value = jnp.where(offset == -1, -8.0, value)
    value = jnp.where(offset == 2, -1.0, value)
    value = jnp.where(offset == -2, 1.0, value)
    return value


def kernel(
    n, hs, kh, nx,
    slots, d_hbm, a_hbm, out_ref,
    gbuf, pbuf, abuf, apbuf, ebuf, epbuf,
    d_st, dx_st, dr_st, a_st, ax_st, ar_st, e_st, ex_st, er_st,
    run, run_e, sbuf, sbuf_e, rbuf, rbuf_e, radial, axial, slots_e,
    local_d, local_a,
    right_send, right_recv, left_send, left_recv,
    core_send, core_recv, adj_send, adj_recv,
    edge_send, edge_recv, edge_core_send, edge_core_recv, slots_sem,
    slab_send, slab_recv, slab_send_e, slab_recv_e,
):
    me = lax.axis_index("mode")
    my_harm = lax.axis_index("harm")
    core = lax.axis_index("rad")
    per_owner = n // hs
    cells = nx // n
    rows = d_hbm.shape[1]
    chunk = axial.shape[0]
    planes_k = SLOTS * PLANES
    first, last = me == 0, me == n - 1
    low_helper, high_helper = me == 1, me == n - 2

    for k in range(kh):
        pltpu.make_async_copy(d_hbm.at[k], gbuf.at[me, k], local_d.at[k]).start()
    for k in range(kh):
        pltpu.make_async_copy(a_hbm.at[k], abuf.at[k], local_a.at[k]).start()

    barrier = pltpu.get_barrier_semaphore()

    def greet(index, carry):
        q = index // hs
        h = index % hs

        @pl.when(jnp.logical_or(q != me, h != my_harm))
        def _():
            pl.semaphore_signal(barrier, inc=1, device_id={"mode": q, "harm": h}, device_id_type=MESH)

        return carry

    lax.fori_loop(0, n * hs, greet, 0)
    pl.semaphore_signal(barrier, inc=1, device_id={"rad": 1 - core}, device_id_type=MESH)

    row = lax.broadcasted_iota(jnp.int32, (128, 128), 0)
    col = lax.broadcasted_iota(jnp.int32, (128, 128), 1)
    shift = (1 - 2 * core) * 128
    radial[0:128, :] = coefficient(row - col).astype(jnp.bfloat16)
    radial[128:256, :] = coefficient(row - col + shift).astype(jnp.bfloat16)
    row = lax.broadcasted_iota(jnp.int32, (chunk, chunk), 0)
    col = lax.broadcasted_iota(jnp.int32, (chunk, chunk), 1)
    same = (row // nx) == (col // nx)
    axial[...] = jnp.where(same, coefficient(col - row), 0.0).astype(jnp.bfloat16)
    run[...] = jnp.zeros_like(run)
    run_e[...] = jnp.zeros_like(run_e)

    pl.semaphore_wait(barrier, n * hs)

    def remote(src, dst, send, recv, target):
        return pltpu.make_async_remote_copy(
            src_ref=src, dst_ref=dst, send_sem=send, recv_sem=recv,
            device_id=target, device_id_type=MESH)

    other = {"rad": 1 - core}

    def to_right(block, k):
        return remote(gbuf.at[block, k], gbuf.at[block, k],
                      right_send.at[block, k], right_recv.at[block, k], {"mode": me + 1})

    def to_left(block, k):
        return remote(gbuf.at[block, k], gbuf.at[block, k],
                      left_send.at[block, k], left_recv.at[block, k], {"mode": me - 1})

    def to_core(block, k):
        return remote(gbuf.at[block, k], pbuf.at[block, k],
                      core_send.at[block, k], core_recv.at[block, k], other)

    def adjoint_to_core(k):
        return remote(abuf.at[k], apbuf.at[k], adj_send.at[k], adj_recv.at[k], other)

    def edge(k, target):
        return remote(abuf.at[k], ebuf.at[k], edge_send.at[k], edge_recv.at[k], {"mode": target})

    def edge_to_core(k):
        return remote(ebuf.at[k], epbuf.at[k], edge_core_send.at[k], edge_core_recv.at[k], other)

    def edge_slots(target):
        return remote(slots, slots_e, slots_sem.at[0], slots_sem.at[1], {"mode": target})

    for k in range(kh):
        pltpu.make_async_copy(d_hbm.at[k], gbuf.at[me, k], local_d.at[k]).wait()

        @pl.when(me < n - 1)
        def _():
            to_right(me, k).start()

        @pl.when(me > 0)
        def _():
            to_left(me, k).start()

        to_core(me, k).start()

    for k in range(kh):
        pltpu.make_async_copy(a_hbm.at[k], abuf.at[k], local_a.at[k]).wait()
        adjoint_to_core(k).start()

    @pl.when(first)
    def _():
        edge_slots(1).start()

    @pl.when(last)
    def _():
        edge_slots(n - 2).start()

    def prepare(own, partner, plain, along_x, along_r, base):
        def step(i, carry):
            at = pl.ds(pl.multiple_of(i * chunk, chunk), chunk)
            planes = pl.ds(base + i * (chunk // nx), chunk // nx)
            mine = own[at, :]
            both = jnp.concatenate([mine, partner[at, :]], axis=1)
            shape = (chunk // nx, nx, 128)
            plain[planes] = mine.astype(jnp.float32).reshape(shape)
            along_r[planes] = jnp.dot(
                both, radial[...], preferred_element_type=jnp.float32).reshape(shape)
            along_x[planes] = jnp.dot(
                axial[...], mine, preferred_element_type=jnp.float32).reshape(shape)
            return carry

        lax.fori_loop(0, rows // chunk, step, 0)

    def products(table, stop, total, adj, adj_x, adj_r, base):
        def one_mode(m, carry):
            da = base + table[m, stop, 0] * PLANES
            dd = table[m, stop, 1] * PLANES
            for half in range(nx // 8):
                part = pl.ds(half * 8, 8)
                d1r = d_st[dd + 1, part, :]
                d2r = d_st[dd + 2, part, :]
                d1i = d_st[dd + FIELDS + 1, part, :]
                d2i = d_st[dd + FIELDS + 2, part, :]
                a1r = adj[da + 1, part, :]
                a2r = adj[da + 2, part, :]
                a1i = adj[da + FIELDS + 1, part, :]
                a2i = adj[da + FIELDS + 2, part, :]
                for f in range(FIELDS):
                    axr = adj_x[da + f, part, :]
                    axi = adj_x[da + FIELDS + f, part, :]
                    arr = adj_r[da + f, part, :]
                    ari = adj_r[da + FIELDS + f, part, :]
                    dxr = dx_st[dd + f, part, :]
                    dxi = dx_st[dd + FIELDS + f, part, :]
                    drr = dr_st[dd + f, part, :]
                    dri = dr_st[dd + FIELDS + f, part, :]
                    total[m * PLANES + f, part, :] += (
                        ((d1r * axr + d1i * axi) + (d2r * arr + d2i * ari))
                        + ((dxr * a1r + dxi * a1i) + (drr * a2r + dri * a2i)))
                    total[m * PLANES + FIELDS + f, part, :] += (
                        ((d1r * axi - d1i * axr) + (d2r * ari - d2i * arr))
                        + ((dxr * a1i - dxi * a1r) + (drr * a2i - dri * a2r)))
            return carry

        lax.fori_loop(0, SLOTS, one_mode, 0)

    def visit(block, stop, k):
        to_core(block, k).wait_recv()
        prepare(gbuf.at[block, k], pbuf.at[block, k], d_st, dx_st, dr_st, 0)
        products(slots, stop, run, a_st, ax_st, ar_st, k * planes_k)

    def visit_edge(stop, k):
        edge_to_core(k).wait_recv()
        prepare(ebuf.at[k], epbuf.at[k], e_st, ex_st, er_st, 0)
        products(slots_e, stop, run_e, e_st, ex_st, er_st, 0)

    def arrive_chunk(hop, k):
        from_left = me - hop
        from_right = me + hop

        @pl.when(from_left >= 0)
        def _():
            to_right(from_left, k).wait_recv()

            @pl.when(jnp.logical_and(me < n - 1, jnp.logical_or(me < n - 2, from_left > 0)))
            def _():
                to_right(from_left, k).start()

            to_core(from_left, k).start()

        @pl.when(from_right < n)
        def _():
            to_left(from_right, k).wait_recv()

            @pl.when(jnp.logical_and(me > 0, jnp.logical_or(me > 1, from_right < n - 1)))
            def _():
                to_left(from_right, k).start()

            to_core(from_right, k).start()

        @pl.when(jnp.logical_and(hop == 1, first))
        def _():
            to_right(me, k).wait_send()
            edge(k, 1).start()

        @pl.when(jnp.logical_and(hop == 1, last))
        def _():
            to_left(me, k).wait_send()
            edge(k, n - 2).start()

        @pl.when(jnp.logical_and(hop == n - 2, jnp.logical_or(low_helper, high_helper)))
        def _():
            edge(k, me).wait_recv()
            edge_to_core(k).start()

    def visit_chunk(hop, k):
        @pl.when(me - hop >= 0)
        def _():
            visit(me - hop, hop, k)

            @pl.when(jnp.logical_and(hop == n - 2, high_helper))
            def _():
                visit_edge(n - 1, k)

        @pl.when(me + hop < n)
        def _():
            visit(me + hop, n - hop, k)

            @pl.when(jnp.logical_and(hop == n - 2, low_helper))
            def _():
                visit_edge(1, k)

    def own_chunk(k, carry):
        adjoint_to_core(k).wait_recv()
        prepare(abuf.at[k], apbuf.at[k], a_st, ax_st, ar_st, k * planes_k)
        visit(me, 0, k)
        return carry

    lax.fori_loop(0, kh, own_chunk, 0)

    @pl.when(jnp.logical_or(low_helper, high_helper))
    def _():
        edge_slots(me).wait_recv()

    count = (n - 2) * kh

    def steps(i, carry):
        @pl.when(i < count)
        def _():
            arrive_chunk(1 + i // kh, i % kh)

        @pl.when(i > 0)
        def _():
            visit_chunk(1 + (i - 1) // kh, (i - 1) % kh)

        return carry

    lax.fori_loop(0, count + 1, steps, 0)

    scale = 1.0 / (12.0 * math.sqrt(8.0 * n * HARMS))
    owner = me // per_owner
    place = me % per_owner
    helper = jnp.logical_or(low_helper, high_helper)
    side = jnp.where(low_helper, 0, 1)
    owner_e = jnp.where(low_helper, 0, hs - 1)

    def slab(q, h, i):
        return remote(sbuf.at[q], rbuf.at[h * per_owner + i],
                      slab_send.at[q], slab_recv.at[h * per_owner + i],
                      {"mode": q, "harm": owner})

    def slab_e(q, h, i):
        return remote(sbuf_e.at[q], rbuf_e.at[i * hs + h],
                      slab_send_e.at[q], slab_recv_e.at[i * hs + h],
                      {"mode": q, "harm": owner_e})

    def each_target(act, act_e):
        def step(q, carry):
            @pl.when(jnp.logical_or(q != me, owner != my_harm))
            def _():
                act(slab(q, my_harm, place))

            @pl.when(jnp.logical_and(helper, jnp.logical_or(q != me, owner_e != my_harm)))
            def _():
                act_e(slab_e(q, my_harm, side))

            return carry

        lax.fori_loop(0, n, step, 0)

    for q in range(n):
        sbuf[q] = run[:, q * cells:(q + 1) * cells, :] * scale

    @pl.when(helper)
    def _():
        for q in range(n):
            sbuf_e[q] = run_e[:, q * cells:(q + 1) * cells, :] * scale

    each_target(lambda copy: copy.start(), lambda copy: copy.start())

    @pl.when(owner == my_harm)
    def _():
        rbuf[my_harm * per_owner + place] = sbuf[me]

    @pl.when(jnp.logical_and(helper, owner_e == my_harm))
    def _():
        rbuf_e[side * hs + my_harm] = sbuf_e[me]

    def arrive(index, carry):
        h = index // per_owner
        i = index % per_owner
        mine = jnp.logical_and(h == my_harm, my_harm * per_owner + i == me)

        @pl.when(jnp.logical_not(mine))
        def _():
            slab(0, h, i).wait_recv()

        return carry

    lax.fori_loop(0, hs * per_owner, arrive, 0)
    for i in range(per_owner):
        total = rbuf[i]
        for h in range(1, hs):
            total = total + rbuf[h * per_owner + i]
        out_ref[i] = total

    for i, source, holder, spot in ((0, 1, 0, 0), (1, n - 2, hs - 1, per_owner - 1)):
        @pl.when(my_harm == holder)
        def _(i=i, source=source, spot=spot):
            def wait_edge(h, carry):
                @pl.when(jnp.logical_or(h != my_harm, me != source))
                def _():
                    slab_e(0, h, i).wait_recv()

                return carry

            lax.fori_loop(0, hs, wait_edge, 0)
            total = out_ref[spot]
            for h in range(hs):
                total = total + rbuf_e[i * hs + h]
            out_ref[spot] = total

    each_target(lambda copy: copy.wait_send(), lambda copy: copy.wait_send())

    def drain(i, carry):
        block = i // kh
        k = i % kh

        @pl.when(jnp.logical_not(jnp.logical_or(
            jnp.logical_and(first, block == n - 1), jnp.logical_and(last, block == 0))))
        def _():
            to_core(block, k).wait_send()

        @pl.when(jnp.logical_and(
            jnp.logical_and(block <= me, me < n - 1),
            jnp.logical_and(
                jnp.logical_or(me < n - 2, block > 0),
                jnp.logical_not(first))))
        def _():
            to_right(block, k).wait_send()

        @pl.when(jnp.logical_and(
            jnp.logical_and(block >= me, me > 0),
            jnp.logical_and(
                jnp.logical_or(me > 1, block < n - 1),
                jnp.logical_not(last))))
        def _():
            to_left(block, k).wait_send()

        return carry

    lax.fori_loop(0, n * kh, drain, 0)

    def drain_adjoint(k, carry):
        adjoint_to_core(k).wait_send()

        @pl.when(jnp.logical_or(first, last))
        def _():
            edge(k, me).wait_send()

        @pl.when(helper)
        def _():
            edge_to_core(k).wait_send()

        return carry

    lax.fori_loop(0, kh, drain_adjoint, 0)

    @pl.when(jnp.logical_or(first, last))
    def _():
        edge_slots(me).wait_send()


def body(hs, direct_field, adjoint_field, triad_slots):
    n = triad_slots.shape[1]
    kh = direct_field.shape[0]
    nx = direct_field.shape[4]
    planes = SLOTS * PLANES
    rows = planes * nx
    chunk = 128
    cells = nx // n
    per_owner = n // hs
    f32, bf16 = jnp.float32, jnp.bfloat16
    dma = pltpu.SemaphoreType.DMA
    slab_shape = (planes, cells, 128)
    out = pl.pallas_call(
        functools.partial(kernel, n, hs, kh, nx),
        out_shape=jax.ShapeDtypeStruct((per_owner,) + slab_shape, f32),
        in_specs=[pl.BlockSpec(memory_space=pltpu.SMEM)] + [pl.BlockSpec(memory_space=pl.ANY)] * 2,
        out_specs=pl.BlockSpec(memory_space=pltpu.VMEM),
        scratch_shapes=[pltpu.VMEM((n, kh, rows, 128), bf16)] * 2
        + [pltpu.VMEM((kh, rows, 128), bf16)] * 4
        + [pltpu.VMEM((planes, nx, 128), f32)] * 3
        + [pltpu.VMEM((kh * planes, nx, 128), f32)] * 3
        + [pltpu.VMEM((planes, nx, 128), f32)] * 5
        + [
            pltpu.VMEM((n,) + slab_shape, f32),
            pltpu.VMEM((n,) + slab_shape, f32),
            pltpu.VMEM((hs * per_owner,) + slab_shape, f32),
            pltpu.VMEM((2 * hs,) + slab_shape, f32),
            pltpu.VMEM((256, 128), bf16),
            pltpu.VMEM((chunk, chunk), bf16),
            pltpu.SMEM(triad_slots.shape, jnp.int32),
            dma((kh,)), dma((kh,)),
            dma((n, kh)), dma((n, kh)), dma((n, kh)), dma((n, kh)),
            dma((n, kh)), dma((n, kh)), dma((kh,)), dma((kh,)),
            dma((kh,)), dma((kh,)), dma((kh,)), dma((kh,)), dma((2,)),
            dma((n,)), dma((hs * per_owner,)), dma((n,)), dma((2 * hs,)),
        ],
        compiler_params=pltpu.CompilerParams(
            collective_id=0, has_side_effects=True, vmem_limit_bytes=56 << 20),
    )(
        triad_slots,
        direct_field.reshape(kh, rows, 128),
        adjoint_field.reshape(kh, rows, 128),
    )
    return out.reshape(per_owner * SLOTS, 2, FIELDS, cells, 128)


def solution(mesh):
    return jax.shard_map(
        functools.partial(body, mesh.shape["harm"]),
        mesh=mesh,
        in_specs=(
            P(("case", "harm"), "mode", None, None, None, "rad"),
            P(("case", "harm"), "mode", None, None, None, "rad"),
            P("mode", None, None),
        ),
        out_specs=P(("case", "harm"), None, None, "mode", "rad"),
        check_vma=False,
    )
```

```python
import functools
import math

import jax
import jax.numpy as jnp
from jax import lax
from jax.experimental import pallas as pl
from jax.experimental.pallas import tpu as pltpu
from jax.sharding import PartitionSpec as P

HARMS = 8
SLOTS = 4
FIELDS = 5
PLANES = 2 * FIELDS
MESH = pl.DeviceIdType.MESH


def coefficient(offset):
    value = jnp.where(offset == 1, 8.0, 0.0)
    value = jnp.where(offset == -1, -8.0, value)
    value = jnp.where(offset == 2, -1.0, value)
    value = jnp.where(offset == -2, 1.0, value)
    return value


def kernel(
    n, hs, kh, nx,
    slots, d_hbm, a_hbm, out_ref,
    gbuf, pbuf, abuf, apbuf, ebuf, epbuf,
    d_st, dx_st, dr_st, a_st, ax_st, ar_st, e_st, ex_st, er_st,
    run, run_e, sbuf, sbuf_e, rbuf, rbuf_e, radial, axial, slots_e,
    local_d, local_a,
    right_send, right_recv, left_send, left_recv,
    core_send, core_recv, adj_send, adj_recv,
    edge_send, edge_recv, edge_core_send, edge_core_recv, slots_sem,
    slab_send, slab_recv, slab_send_e, slab_recv_e,
):
    me = lax.axis_index("mode")
    my_harm = lax.axis_index("harm")
    core = lax.axis_index("rad")
    per_owner = n // hs
    cells = nx // n
    rows = d_hbm.shape[1]
    chunk = axial.shape[0]
    planes_k = SLOTS * PLANES
    first, last = me == 0, me == n - 1
    low_helper, high_helper = me == 1, me == n - 2

    for k in range(kh):
        pltpu.make_async_copy(d_hbm.at[k], gbuf.at[me, k], local_d.at[k]).start()
    for k in range(kh):
        pltpu.make_async_copy(a_hbm.at[k], abuf.at[k], local_a.at[k]).start()

    barrier = pltpu.get_barrier_semaphore()

    def greet(index, carry):
        q = index // hs
        h = index % hs

        @pl.when(jnp.logical_or(q != me, h != my_harm))
        def _():
            pl.semaphore_signal(barrier, inc=1, device_id={"mode": q, "harm": h}, device_id_type=MESH)

        return carry

    lax.fori_loop(0, n * hs, greet, 0)
    pl.semaphore_signal(barrier, inc=1, device_id={"rad": 1 - core}, device_id_type=MESH)

    row = lax.broadcasted_iota(jnp.int32, (128, 128), 0)
    col = lax.broadcasted_iota(jnp.int32, (128, 128), 1)
    shift = (1 - 2 * core) * 128
    radial[0:128, :] = coefficient(row - col).astype(jnp.bfloat16)
    radial[128:256, :] = coefficient(row - col + shift).astype(jnp.bfloat16)
    row = lax.broadcasted_iota(jnp.int32, (chunk, chunk), 0)
    col = lax.broadcasted_iota(jnp.int32, (chunk, chunk), 1)
    same = (row // nx) == (col // nx)
    axial[...] = jnp.where(same, coefficient(col - row), 0.0).astype(jnp.bfloat16)
    run[...] = jnp.zeros_like(run)
    run_e[...] = jnp.zeros_like(run_e)

    pl.semaphore_wait(barrier, n * hs)

    def remote(src, dst, send, recv, target):
        return pltpu.make_async_remote_copy(
            src_ref=src, dst_ref=dst, send_sem=send, recv_sem=recv,
            device_id=target, device_id_type=MESH)

    other = {"rad": 1 - core}

    def to_right(block, k):
        return remote(gbuf.at[block, k], gbuf.at[block, k],
                      right_send.at[block, k], right_recv.at[block, k], {"mode": me + 1})

    def to_left(block, k):
        return remote(gbuf.at[block, k], gbuf.at[block, k],
                      left_send.at[block, k], left_recv.at[block, k], {"mode": me - 1})

    def to_core(block, k):
        return remote(gbuf.at[block, k], pbuf.at[block, k],
                      core_send.at[block, k], core_recv.at[block, k], other)

    def adjoint_to_core(k):
        return remote(abuf.at[k], apbuf.at[k], adj_send.at[k], adj_recv.at[k], other)

    def edge(k, target):
        return remote(abuf.at[k], ebuf.at[k], edge_send.at[k], edge_recv.at[k], {"mode": target})

    def edge_to_core(k):
        return remote(ebuf.at[k], epbuf.at[k], edge_core_send.at[k], edge_core_recv.at[k], other)

    def edge_slots(target):
        return remote(slots, slots_e, slots_sem.at[0], slots_sem.at[1], {"mode": target})

    for k in range(kh):
        pltpu.make_async_copy(d_hbm.at[k], gbuf.at[me, k], local_d.at[k]).wait()

        @pl.when(me < n - 1)
        def _():
            to_right(me, k).start()

        @pl.when(me > 0)
        def _():
            to_left(me, k).start()

        to_core(me, k).start()

    for k in range(kh):
        pltpu.make_async_copy(a_hbm.at[k], abuf.at[k], local_a.at[k]).wait()
        adjoint_to_core(k).start()

    @pl.when(first)
    def _():
        edge_slots(1).start()

    @pl.when(last)
    def _():
        edge_slots(n - 2).start()

    def prepare(own, partner, plain, along_x, along_r, base):
        def step(i, carry):
            at = pl.ds(pl.multiple_of(i * chunk, chunk), chunk)
            planes = pl.ds(base + i * (chunk // nx), chunk // nx)
            mine = own[at, :]
            both = jnp.concatenate([mine, partner[at, :]], axis=1)
            shape = (chunk // nx, nx, 128)
            plain[planes] = mine.astype(jnp.float32).reshape(shape)
            along_r[planes] = jnp.dot(
                both, radial[...], preferred_element_type=jnp.float32).reshape(shape)
            along_x[planes] = jnp.dot(
                axial[...], mine, preferred_element_type=jnp.float32).reshape(shape)
            return carry

        lax.fori_loop(0, rows // chunk, step, 0)

    def products(table, stop, total, adj, adj_x, adj_r, base):
        def one_mode(m, carry):
            da = base + table[m, 0, stop] * PLANES
            dd = table[m, 1, stop] * PLANES
            for half in range(nx // 8):
                part = pl.ds(half * 8, 8)
                d1r = d_st[dd + 1, part, :]
                d2r = d_st[dd + 2, part, :]
                d1i = d_st[dd + FIELDS + 1, part, :]
                d2i = d_st[dd + FIELDS + 2, part, :]
                a1r = adj[da + 1, part, :]
                a2r = adj[da + 2, part, :]
                a1i = adj[da + FIELDS + 1, part, :]
                a2i = adj[da + FIELDS + 2, part, :]
                for f in range(FIELDS):
                    axr = adj_x[da + f, part, :]
                    axi = adj_x[da + FIELDS + f, part, :]
                    arr = adj_r[da + f, part, :]
                    ari = adj_r[da + FIELDS + f, part, :]
                    dxr = dx_st[dd + f, part, :]
                    dxi = dx_st[dd + FIELDS + f, part, :]
                    drr = dr_st[dd + f, part, :]
                    dri = dr_st[dd + FIELDS + f, part, :]
                    total[m * PLANES + f, part, :] += (
                        ((d1r * axr + d1i * axi) + (d2r * arr + d2i * ari))
                        + ((dxr * a1r + dxi * a1i) + (drr * a2r + dri * a2i)))
                    total[m * PLANES + FIELDS + f, part, :] += (
                        ((d1r * axi - d1i * axr) + (d2r * ari - d2i * arr))
                        + ((dxr * a1i - dxi * a1r) + (drr * a2i - dri * a2r)))
            return carry

        lax.fori_loop(0, SLOTS, one_mode, 0)

    def visit(block, stop, k):
        to_core(block, k).wait_recv()
        prepare(gbuf.at[block, k], pbuf.at[block, k], d_st, dx_st, dr_st, 0)
        products(slots, stop, run, a_st, ax_st, ar_st, k * planes_k)

    def visit_edge(stop, k):
        edge_to_core(k).wait_recv()
        prepare(ebuf.at[k], epbuf.at[k], e_st, ex_st, er_st, 0)
        products(slots_e, stop, run_e, e_st, ex_st, er_st, 0)

    def arrive_chunk(hop, k):
        from_left = me - hop
        from_right = me + hop

        @pl.when(from_left >= 0)
        def _():
            to_right(from_left, k).wait_recv()

            @pl.when(jnp.logical_and(me < n - 1, jnp.logical_or(me < n - 2, from_left > 0)))
            def _():
                to_right(from_left, k).start()

            to_core(from_left, k).start()

        @pl.when(from_right < n)
        def _():
            to_left(from_right, k).wait_recv()

            @pl.when(jnp.logical_and(me > 0, jnp.logical_or(me > 1, from_right < n - 1)))
            def _():
                to_left(from_right, k).start()

            to_core(from_right, k).start()

        @pl.when(jnp.logical_and(hop == 1, first))
        def _():
            to_right(me, k).wait_send()
            edge(k, 1).start()

        @pl.when(jnp.logical_and(hop == 1, last))
        def _():
            to_left(me, k).wait_send()
            edge(k, n - 2).start()

        @pl.when(jnp.logical_and(hop == n - 2, jnp.logical_or(low_helper, high_helper)))
        def _():
            edge(k, me).wait_recv()
            edge_to_core(k).start()

    def visit_chunk(hop, k):
        @pl.when(me - hop >= 0)
        def _():
            visit(me - hop, hop, k)

            @pl.when(jnp.logical_and(hop == n - 2, high_helper))
            def _():
                visit_edge(n - 1, k)

        @pl.when(me + hop < n)
        def _():
            visit(me + hop, n - hop, k)

            @pl.when(jnp.logical_and(hop == n - 2, low_helper))
            def _():
                visit_edge(1, k)

    def own_chunk(k, carry):
        adjoint_to_core(k).wait_recv()
        prepare(abuf.at[k], apbuf.at[k], a_st, ax_st, ar_st, k * planes_k)
        visit(me, 0, k)
        return carry

    lax.fori_loop(0, kh, own_chunk, 0)

    @pl.when(jnp.logical_or(low_helper, high_helper))
    def _():
        edge_slots(me).wait_recv()

    count = (n - 2) * kh

    def steps(i, carry):
        @pl.when(i < count)
        def _():
            arrive_chunk(1 + i // kh, i % kh)

        @pl.when(i > 0)
        def _():
            visit_chunk(1 + (i - 1) // kh, (i - 1) % kh)

        return carry

    lax.fori_loop(0, count + 1, steps, 0)

    scale = 1.0 / (12.0 * math.sqrt(8.0 * n * HARMS))
    owner = me // per_owner
    place = me % per_owner
    helper = jnp.logical_or(low_helper, high_helper)
    side = jnp.where(low_helper, 0, 1)
    owner_e = jnp.where(low_helper, 0, hs - 1)

    def slab(q, h, i):
        return remote(sbuf.at[q], rbuf.at[h * per_owner + i],
                      slab_send.at[q], slab_recv.at[h * per_owner + i],
                      {"mode": q, "harm": owner})

    def slab_e(q, h, i):
        return remote(sbuf_e.at[q], rbuf_e.at[i * hs + h],
                      slab_send_e.at[q], slab_recv_e.at[i * hs + h],
                      {"mode": q, "harm": owner_e})

    def each_target(act, act_e):
        def step(q, carry):
            @pl.when(jnp.logical_or(q != me, owner != my_harm))
            def _():
                act(slab(q, my_harm, place))

            @pl.when(jnp.logical_and(helper, jnp.logical_or(q != me, owner_e != my_harm)))
            def _():
                act_e(slab_e(q, my_harm, side))

            return carry

        lax.fori_loop(0, n, step, 0)

    for q in range(n):
        sbuf[q] = run[:, q * cells:(q + 1) * cells, :] * scale

    @pl.when(helper)
    def _():
        for q in range(n):
            sbuf_e[q] = run_e[:, q * cells:(q + 1) * cells, :] * scale

    each_target(lambda copy: copy.start(), lambda copy: copy.start())

    @pl.when(owner == my_harm)
    def _():
        rbuf[my_harm * per_owner + place] = sbuf[me]

    @pl.when(jnp.logical_and(helper, owner_e == my_harm))
    def _():
        rbuf_e[side * hs + my_harm] = sbuf_e[me]

    def arrive(index, carry):
        h = index // per_owner
        i = index % per_owner
        mine = jnp.logical_and(h == my_harm, my_harm * per_owner + i == me)

        @pl.when(jnp.logical_not(mine))
        def _():
            slab(0, h, i).wait_recv()

        return carry

    lax.fori_loop(0, hs * per_owner, arrive, 0)
    for i in range(per_owner):
        total = rbuf[i]
        for h in range(1, hs):
            total = total + rbuf[h * per_owner + i]
        out_ref[i] = total

    for i, source, holder, spot in ((0, 1, 0, 0), (1, n - 2, hs - 1, per_owner - 1)):
        @pl.when(my_harm == holder)
        def _(i=i, source=source, spot=spot):
            def wait_edge(h, carry):
                @pl.when(jnp.logical_or(h != my_harm, me != source))
                def _():
                    slab_e(0, h, i).wait_recv()

                return carry

            lax.fori_loop(0, hs, wait_edge, 0)
            total = out_ref[spot]
            for h in range(hs):
                total = total + rbuf_e[i * hs + h]
            out_ref[spot] = total

    each_target(lambda copy: copy.wait_send(), lambda copy: copy.wait_send())

    def drain(i, carry):
        block = i // kh
        k = i % kh

        @pl.when(jnp.logical_not(jnp.logical_or(
            jnp.logical_and(first, block == n - 1), jnp.logical_and(last, block == 0))))
        def _():
            to_core(block, k).wait_send()

        @pl.when(jnp.logical_and(
            jnp.logical_and(block <= me, me < n - 1),
            jnp.logical_and(
                jnp.logical_or(me < n - 2, block > 0),
                jnp.logical_not(first))))
        def _():
            to_right(block, k).wait_send()

        @pl.when(jnp.logical_and(
            jnp.logical_and(block >= me, me > 0),
            jnp.logical_and(
                jnp.logical_or(me > 1, block < n - 1),
                jnp.logical_not(last))))
        def _():
            to_left(block, k).wait_send()

        return carry

    lax.fori_loop(0, n * kh, drain, 0)

    def drain_adjoint(k, carry):
        adjoint_to_core(k).wait_send()

        @pl.when(jnp.logical_or(first, last))
        def _():
            edge(k, me).wait_send()

        @pl.when(helper)
        def _():
            edge_to_core(k).wait_send()

        return carry

    lax.fori_loop(0, kh, drain_adjoint, 0)

    @pl.when(jnp.logical_or(first, last))
    def _():
        edge_slots(me).wait_send()


def body(hs, direct_field, adjoint_field, triad_slots):
    n = triad_slots.shape[1]
    kh = direct_field.shape[0]
    nx = direct_field.shape[4]
    planes = SLOTS * PLANES
    rows = planes * nx
    chunk = 128
    cells = nx // n
    per_owner = n // hs
    f32, bf16 = jnp.float32, jnp.bfloat16
    dma = pltpu.SemaphoreType.DMA
    slab_shape = (planes, cells, 128)
    out = pl.pallas_call(
        functools.partial(kernel, n, hs, kh, nx),
        out_shape=jax.ShapeDtypeStruct((per_owner,) + slab_shape, f32),
        in_specs=[pl.BlockSpec(memory_space=pltpu.SMEM)] + [pl.BlockSpec(memory_space=pltpu.HBM)] * 2,
        out_specs=pl.BlockSpec(memory_space=pltpu.VMEM),
        scratch_shapes=[pltpu.VMEM((n, kh, rows, 128), bf16)] * 2
        + [pltpu.VMEM((kh, rows, 128), bf16)] * 4
        + [pltpu.VMEM((planes, nx, 128), f32)] * 3
        + [pltpu.VMEM((kh * planes, nx, 128), f32)] * 3
        + [pltpu.VMEM((planes, nx, 128), f32)] * 5
        + [
            pltpu.VMEM((n,) + slab_shape, f32),
            pltpu.VMEM((n,) + slab_shape, f32),
            pltpu.VMEM((hs * per_owner,) + slab_shape, f32),
            pltpu.VMEM((2 * hs,) + slab_shape, f32),
            pltpu.VMEM((256, 128), bf16),
            pltpu.VMEM((chunk, chunk), bf16),
            pltpu.SMEM((SLOTS, 2, n), jnp.int32),
            dma((kh,)), dma((kh,)),
            dma((n, kh)), dma((n, kh)), dma((n, kh)), dma((n, kh)),
            dma((n, kh)), dma((n, kh)), dma((kh,)), dma((kh,)),
            dma((kh,)), dma((kh,)), dma((kh,)), dma((kh,)), dma((2,)),
            dma((n,)), dma((hs * per_owner,)), dma((n,)), dma((2 * hs,)),
        ],
        compiler_params=pltpu.CompilerParams(
            collective_id=0, has_side_effects=True, vmem_limit_bytes=56_000_000),
    )(
        jnp.transpose(triad_slots, (0, 2, 1)),
        direct_field.reshape(kh, rows, 128),
        adjoint_field.reshape(kh, rows, 128),
    )
    return out.reshape(per_owner * SLOTS, 2, FIELDS, cells, 128)


def solution(mesh):
    return jax.shard_map(
        functools.partial(body, mesh.shape["harm"]),
        mesh=mesh,
        in_specs=(
            P(("case", "harm"), "mode", None, None, None, "rad"),
            P(("case", "harm"), "mode", None, None, None, "rad"),
            P("mode", None, None),
        ),
        out_specs=P(("case", "harm"), None, None, "mode", "rad"),
        check_vma=False,
    )
```

```python
import functools
import math

import jax
import jax.numpy as jnp
from jax import lax
from jax.experimental import pallas as pl
from jax.experimental.pallas import tpu as pltpu
from jax.sharding import PartitionSpec as P

HARMS = 8
SLOTS = 4
FIELDS = 5
ORDER = (1, 2, 0, 3, 4)
MESH = pl.DeviceIdType.MESH


def coefficient(offset):
    value = jnp.where(offset == 1, 8.0, 0.0)
    value = jnp.where(offset == -1, -8.0, value)
    value = jnp.where(offset == 2, -1.0, value)
    value = jnp.where(offset == -2, 1.0, value)
    return value


def kernel(
    n, hs, kh, nx,
    slots, d_hbm, a_hbm, out_ref,
    gbuf, pbuf, abuf, apbuf, ebuf, epbuf,
    d_st, dx_st, dr_st, f_st, fx_st, fr_st, a_st, ax_st, ar_st, e_st, ex_st, er_st,
    run, run_e, sbuf, sbuf_e, rbuf, rbuf_e, radial, axial, slots_e,
    local_d, local_a,
    right_send, right_recv, left_send, left_recv,
    core_send, core_recv, adj_send, adj_recv,
    edge_send, edge_recv, edge_core_send, edge_core_recv, slots_sem,
    slab_send, slab_recv, slab_send_e, slab_recv_e,
):
    me = lax.axis_index("mode")
    my_harm = lax.axis_index("harm")
    core = lax.axis_index("rad")
    per_owner = n // hs
    cells = nx // n
    wide = d_hbm.shape[0]
    chunk = axial.shape[0]
    first, last = me == 0, me == n - 1
    low_helper, high_helper = me == 1, me == n - 2

    for k in range(FIELDS):
        pltpu.make_async_copy(d_hbm.at[:, ORDER[k]], gbuf.at[me, k], local_d.at[k]).start()
    for k in range(FIELDS):
        pltpu.make_async_copy(a_hbm.at[:, ORDER[k]], abuf.at[k], local_a.at[k]).start()

    barrier = pltpu.get_barrier_semaphore()

    def greet(index, carry):
        q = index // hs
        h = index % hs

        @pl.when(jnp.logical_or(q != me, h != my_harm))
        def _():
            pl.semaphore_signal(barrier, inc=1, device_id={"mode": q, "harm": h}, device_id_type=MESH)

        return carry

    lax.fori_loop(0, n * hs, greet, 0)
    pl.semaphore_signal(barrier, inc=1, device_id={"rad": 1 - core}, device_id_type=MESH)

    row = lax.broadcasted_iota(jnp.int32, (128, 128), 0)
    col = lax.broadcasted_iota(jnp.int32, (128, 128), 1)
    shift = (1 - 2 * core) * 128
    radial[0:128, :] = coefficient(row - col).astype(jnp.bfloat16)
    radial[128:256, :] = coefficient(row - col + shift).astype(jnp.bfloat16)
    row = lax.broadcasted_iota(jnp.int32, (chunk, chunk), 0)
    col = lax.broadcasted_iota(jnp.int32, (chunk, chunk), 1)
    same = (row // nx) == (col // nx)
    axial[...] = jnp.where(same, coefficient(col - row), 0.0).astype(jnp.bfloat16)
    run[...] = jnp.zeros_like(run)
    run_e[...] = jnp.zeros_like(run_e)

    pl.semaphore_wait(barrier, n * hs)

    def remote(src, dst, send, recv, target):
        return pltpu.make_async_remote_copy(
            src_ref=src, dst_ref=dst, send_sem=send, recv_sem=recv,
            device_id=target, device_id_type=MESH)

    other = {"rad": 1 - core}

    def to_right(block, k):
        return remote(gbuf.at[block, k], gbuf.at[block, k],
                      right_send.at[block, k], right_recv.at[block, k], {"mode": me + 1})

    def to_left(block, k):
        return remote(gbuf.at[block, k], gbuf.at[block, k],
                      left_send.at[block, k], left_recv.at[block, k], {"mode": me - 1})

    def to_core(block, k):
        return remote(gbuf.at[block, k], pbuf.at[block, k],
                      core_send.at[block, k], core_recv.at[block, k], other)

    def adjoint_to_core(k):
        return remote(abuf.at[k], apbuf.at[k], adj_send.at[k], adj_recv.at[k], other)

    def edge(k, target):
        return remote(abuf.at[k], ebuf.at[k], edge_send.at[k], edge_recv.at[k], {"mode": target})

    def edge_to_core(k):
        return remote(ebuf.at[k], epbuf.at[k], edge_core_send.at[k], edge_core_recv.at[k], other)

    def edge_slots(target):
        return remote(slots, slots_e, slots_sem.at[0], slots_sem.at[1], {"mode": target})

    for k in range(FIELDS):
        pltpu.make_async_copy(d_hbm.at[:, ORDER[k]], gbuf.at[me, k], local_d.at[k]).wait()

        @pl.when(me < n - 1)
        def _():
            to_right(me, k).start()

        @pl.when(me > 0)
        def _():
            to_left(me, k).start()

        to_core(me, k).start()

    for k in range(FIELDS):
        pltpu.make_async_copy(a_hbm.at[:, ORDER[k]], abuf.at[k], local_a.at[k]).wait()
        adjoint_to_core(k).start()

    @pl.when(first)
    def _():
        edge_slots(1).start()

    @pl.when(last)
    def _():
        edge_slots(n - 2).start()

    def prepare(own, partner, plain, along_x, along_r, k):
        group = chunk // nx

        def step(i, carry):
            at = pl.ds(i * group, group)
            to = pl.ds(k * wide + i * group, group)
            mine = own[at].reshape(chunk, 128)
            both = jnp.concatenate([mine, partner[at].reshape(chunk, 128)], axis=1)
            shape = (group, nx, 128)

            @pl.when(k < 2)
            def _():
                plain[to] = mine.astype(jnp.float32).reshape(shape)

            along_r[to] = jnp.dot(
                both, radial[...], preferred_element_type=jnp.float32).reshape(shape)
            along_x[to] = jnp.dot(
                axial[...], mine, preferred_element_type=jnp.float32).reshape(shape)
            return carry

        lax.fori_loop(0, wide // group, step, 0)

    def products(table, stop, total, dirs, adjs, k):
        d_pl, d_x, d_r = dirs
        a_pl, a_x, a_r = adjs

        def one_mode(m, carry):
            da = table[m, 0, stop] * 2
            dd = table[m, 1, stop] * 2
            for half in range(nx // 8):
                part = pl.ds(half * 8, 8)
                real = total[(k * SLOTS + m) * 2, part, :]
                imag = total[(k * SLOTS + m) * 2 + 1, part, :]
                for c in range(kh):
                    ia = c * SLOTS * 2 + da
                    id_ = c * SLOTS * 2 + dd
                    d1r = d_pl[id_, part, :]
                    d1i = d_pl[id_ + 1, part, :]
                    d2r = d_pl[wide + id_, part, :]
                    d2i = d_pl[wide + id_ + 1, part, :]
                    a1r = a_pl[ia, part, :]
                    a1i = a_pl[ia + 1, part, :]
                    a2r = a_pl[wide + ia, part, :]
                    a2i = a_pl[wide + ia + 1, part, :]
                    axr = a_x[k * wide + ia, part, :]
                    axi = a_x[k * wide + ia + 1, part, :]
                    arr = a_r[k * wide + ia, part, :]
                    ari = a_r[k * wide + ia + 1, part, :]
                    dxr = d_x[k * wide + id_, part, :]
                    dxi = d_x[k * wide + id_ + 1, part, :]
                    drr = d_r[k * wide + id_, part, :]
                    dri = d_r[k * wide + id_ + 1, part, :]
                    real = real + (
                        ((d1r * axr + d1i * axi) + (d2r * arr + d2i * ari))
                        + ((dxr * a1r + dxi * a1i) + (drr * a2r + dri * a2i)))
                    imag = imag + (
                        ((d1r * axi - d1i * axr) + (d2r * ari - d2i * arr))
                        + ((dxr * a1i - dxi * a1r) + (drr * a2i - dri * a2r)))
                total[(k * SLOTS + m) * 2, part, :] = real
                total[(k * SLOTS + m) * 2 + 1, part, :] = imag
            return carry

        lax.fori_loop(0, SLOTS, one_mode, 0)

    def ready(k, act):
        def step(c, carry):
            act(c)
            return carry

        low = jnp.where(k == 0, 1, jnp.where(k == 1, 0, k))
        lax.fori_loop(low, k + 1, step, 0)

    left_side = (d_st, dx_st, dr_st)
    right_side = (f_st, fx_st, fr_st)
    own_adjoint = (a_st, ax_st, ar_st)
    edge_adjoint = (e_st, ex_st, er_st)

    def visit(block, stop, k, side):
        to_core(block, k).wait_recv()
        prepare(gbuf.at[block, k], pbuf.at[block, k], *side, k)
        ready(k, lambda c: products(slots, stop, run, side, own_adjoint, c))

    def visit_edge(stop, k, side):
        edge_to_core(k).wait_recv()
        prepare(ebuf.at[k], epbuf.at[k], *edge_adjoint, k)
        ready(k, lambda c: products(slots_e, stop, run_e, side, edge_adjoint, c))

    def arrive_chunk(hop, k):
        from_left = me - hop
        from_right = me + hop

        @pl.when(from_left >= 0)
        def _():
            to_right(from_left, k).wait_recv()

            @pl.when(jnp.logical_and(me < n - 1, jnp.logical_or(me < n - 2, from_left > 0)))
            def _():
                to_right(from_left, k).start()

            to_core(from_left, k).start()

        @pl.when(from_right < n)
        def _():
            to_left(from_right, k).wait_recv()

            @pl.when(jnp.logical_and(me > 0, jnp.logical_or(me > 1, from_right < n - 1)))
            def _():
                to_left(from_right, k).start()

            to_core(from_right, k).start()

        @pl.when(jnp.logical_and(hop == 1, first))
        def _():
            to_right(me, k).wait_send()
            edge(k, 1).start()

        @pl.when(jnp.logical_and(hop == 1, last))
        def _():
            to_left(me, k).wait_send()
            edge(k, n - 2).start()

        @pl.when(jnp.logical_and(hop == n - 2, jnp.logical_or(low_helper, high_helper)))
        def _():
            edge(k, me).wait_recv()
            edge_to_core(k).start()

    def visit_chunk(hop, k):
        @pl.when(me - hop >= 0)
        def _():
            visit(me - hop, hop, k, left_side)

            @pl.when(jnp.logical_and(hop == n - 2, high_helper))
            def _():
                visit_edge(n - 1, k, left_side)

        @pl.when(me + hop < n)
        def _():
            visit(me + hop, n - hop, k, right_side)

            @pl.when(jnp.logical_and(hop == n - 2, low_helper))
            def _():
                visit_edge(1, k, right_side)

    scale = 1.0 / (12.0 * math.sqrt(8.0 * n * HARMS))
    owner = me // per_owner
    place = me % per_owner
    helper = jnp.logical_or(low_helper, high_helper)
    side = jnp.where(low_helper, 0, 1)
    owner_e = jnp.where(low_helper, 0, hs - 1)

    def slab(k, q, h, i):
        return remote(sbuf.at[k, q], rbuf.at[k, h * per_owner + i],
                      slab_send.at[k, q], slab_recv.at[k, h * per_owner + i],
                      {"mode": q, "harm": owner})

    def slab_e(k, q, h, i):
        return remote(sbuf_e.at[k, q], rbuf_e.at[k, i * hs + h],
                      slab_send_e.at[k, q], slab_recv_e.at[k, i * hs + h],
                      {"mode": q, "harm": owner_e})

    def each_target(k, act):
        def step(q, carry):
            @pl.when(jnp.logical_or(q != me, owner != my_harm))
            def _():
                act(slab(k, q, my_harm, place))

            @pl.when(jnp.logical_and(helper, jnp.logical_or(q != me, owner_e != my_harm)))
            def _():
                act(slab_e(k, q, my_harm, side))

            return carry

        lax.fori_loop(0, n, step, 0)

    def deliver(k):
        span = pl.ds(k * SLOTS * 2, SLOTS * 2)
        for q in range(n):
            sbuf[k, q] = run[span, q * cells:(q + 1) * cells, :] * scale

        @pl.when(helper)
        def _():
            for q in range(n):
                sbuf_e[k, q] = run_e[span, q * cells:(q + 1) * cells, :] * scale

        each_target(k, lambda copy: copy.start())

        @pl.when(owner == my_harm)
        def _():
            rbuf[k, my_harm * per_owner + place] = sbuf[k, me]

        @pl.when(jnp.logical_and(helper, owner_e == my_harm))
        def _():
            rbuf_e[k, side * hs + my_harm] = sbuf_e[k, me]

    def own_chunk(k, carry):
        adjoint_to_core(k).wait_recv()
        prepare(abuf.at[k], apbuf.at[k], *own_adjoint, k)
        visit(me, 0, k, left_side)
        return carry

    lax.fori_loop(0, FIELDS, own_chunk, 0)

    @pl.when(jnp.logical_or(low_helper, high_helper))
    def _():
        edge_slots(me).wait_recv()

    count = (n - 2) * FIELDS

    def steps(i, carry):
        @pl.when(i < count)
        def _():
            arrive_chunk(1 + i // FIELDS, i % FIELDS)

        @pl.when(i > 0)
        def _():
            visit_chunk(1 + (i - 1) // FIELDS, (i - 1) % FIELDS)

        @pl.when(i > count - FIELDS)
        def _():
            ready(i - 1 - (count - FIELDS), deliver)

        return carry

    lax.fori_loop(0, count + 1, steps, 0)

    def collect(k, carry):
        def arrive(index, inner):
            h = index // per_owner
            i = index % per_owner
            mine = jnp.logical_and(h == my_harm, my_harm * per_owner + i == me)

            @pl.when(jnp.logical_not(mine))
            def _():
                slab(k, 0, h, i).wait_recv()

            return inner

        lax.fori_loop(0, hs * per_owner, arrive, 0)
        field = jnp.where(k < 2, k + 1, jnp.where(k == 2, 0, k))
        for i in range(per_owner):
            total = rbuf[k, i]
            for h in range(1, hs):
                total = total + rbuf[k, h * per_owner + i]
            out_ref[i, :, field] = total

        for i, source, holder, spot in ((0, 1, 0, 0), (1, n - 2, hs - 1, per_owner - 1)):
            @pl.when(my_harm == holder)
            def _(i=i, source=source, spot=spot):
                def wait_edge(h, inner):
                    @pl.when(jnp.logical_or(h != my_harm, me != source))
                    def _():
                        slab_e(k, 0, h, i).wait_recv()

                    return inner

                lax.fori_loop(0, hs, wait_edge, 0)
                total = out_ref[spot, :, field]
                for h in range(hs):
                    total = total + rbuf_e[k, i * hs + h]
                out_ref[spot, :, field] = total

        return carry

    lax.fori_loop(0, FIELDS, collect, 0)

    def drain_slabs(k, carry):
        each_target(k, lambda copy: copy.wait_send())
        return carry

    lax.fori_loop(0, FIELDS, drain_slabs, 0)

    def drain(i, carry):
        block = i // FIELDS
        k = i % FIELDS

        @pl.when(jnp.logical_not(jnp.logical_or(
            jnp.logical_and(first, block == n - 1), jnp.logical_and(last, block == 0))))
        def _():
            to_core(block, k).wait_send()

        @pl.when(jnp.logical_and(
            jnp.logical_and(block <= me, me < n - 1),
            jnp.logical_and(
                jnp.logical_or(me < n - 2, block > 0),
                jnp.logical_not(first))))
        def _():
            to_right(block, k).wait_send()

        @pl.when(jnp.logical_and(
            jnp.logical_and(block >= me, me > 0),
            jnp.logical_and(
                jnp.logical_or(me > 1, block < n - 1),
                jnp.logical_not(last))))
        def _():
            to_left(block, k).wait_send()

        return carry

    lax.fori_loop(0, n * FIELDS, drain, 0)

    def drain_adjoint(k, carry):
        adjoint_to_core(k).wait_send()

        @pl.when(jnp.logical_or(first, last))
        def _():
            edge(k, me).wait_send()

        @pl.when(helper)
        def _():
            edge_to_core(k).wait_send()

        return carry

    lax.fori_loop(0, FIELDS, drain_adjoint, 0)

    @pl.when(jnp.logical_or(first, last))
    def _():
        edge_slots(me).wait_send()


def body(hs, direct_field, adjoint_field, triad_slots):
    n = triad_slots.shape[1]
    kh = direct_field.shape[0]
    nx = direct_field.shape[4]
    wide = kh * SLOTS * 2
    chunk = min(256, wide * nx)
    cells = nx // n
    per_owner = n // hs
    f32, bf16 = jnp.float32, jnp.bfloat16
    dma = pltpu.SemaphoreType.DMA
    slab_shape = (SLOTS * 2, cells, 128)
    block = (FIELDS, wide, nx, 128)
    stage = [
        pltpu.VMEM((2 * wide, nx, 128), f32),
        pltpu.VMEM((FIELDS * wide, nx, 128), f32),
        pltpu.VMEM((FIELDS * wide, nx, 128), f32),
    ]
    c = FIELDS
    out = pl.pallas_call(
        functools.partial(kernel, n, hs, kh, nx),
        out_shape=jax.ShapeDtypeStruct((per_owner, SLOTS * 2, FIELDS, cells, 128), f32),
        in_specs=[pl.BlockSpec(memory_space=pltpu.SMEM)] + [pl.BlockSpec(memory_space=pltpu.HBM)] * 2,
        out_specs=pl.BlockSpec(memory_space=pltpu.VMEM),
        scratch_shapes=[pltpu.VMEM((n,) + block, bf16)] * 2
        + [pltpu.VMEM(block, bf16)] * 4
        + stage * 4
        + [pltpu.VMEM((FIELDS * SLOTS * 2, nx, 128), f32)] * 2
        + [
            pltpu.VMEM((c, n) + slab_shape, f32),
            pltpu.VMEM((c, n) + slab_shape, f32),
            pltpu.VMEM((c, hs * per_owner) + slab_shape, f32),
            pltpu.VMEM((c, 2 * hs) + slab_shape, f32),
            pltpu.VMEM((256, 128), bf16),
            pltpu.VMEM((chunk, chunk), bf16),
            pltpu.SMEM((SLOTS, 2, n), jnp.int32),
            dma((c,)), dma((c,)),
            dma((n, c)), dma((n, c)), dma((n, c)), dma((n, c)),
            dma((n, c)), dma((n, c)), dma((c,)), dma((c,)),
            dma((c,)), dma((c,)), dma((c,)), dma((c,)), dma((2,)),
            dma((c, n)), dma((c, hs * per_owner)), dma((c, n)), dma((c, 2 * hs)),
        ],
        compiler_params=pltpu.CompilerParams(
            collective_id=0, has_side_effects=True, vmem_limit_bytes=56_000_000),
    )(
        jnp.transpose(triad_slots, (0, 2, 1)),
        direct_field.reshape(wide, FIELDS, nx, 128),
        adjoint_field.reshape(wide, FIELDS, nx, 128),
    )
    return out.reshape(per_owner * SLOTS, 2, FIELDS, cells, 128)


def solution(mesh):
    return jax.shard_map(
        functools.partial(body, mesh.shape["harm"]),
        mesh=mesh,
        in_specs=(
            P(("case", "harm"), "mode", None, None, None, "rad"),
            P(("case", "harm"), "mode", None, None, None, "rad"),
            P("mode", None, None),
        ),
        out_specs=P(("case", "harm"), None, None, "mode", "rad"),
        check_vma=False,
    )
```

```python
import functools
import math

import jax
import jax.numpy as jnp
from jax import lax
from jax.experimental import pallas as pl
from jax.experimental.pallas import tpu as pltpu
from jax.sharding import PartitionSpec as P

HARMS = 8
SLOTS = 4
FIELDS = 5
ORDER = (1, 2, 0, 3, 4)
MESH = pl.DeviceIdType.MESH


def coefficient(offset):
    value = jnp.where(offset == 1, 8.0, 0.0)
    value = jnp.where(offset == -1, -8.0, value)
    value = jnp.where(offset == 2, -1.0, value)
    value = jnp.where(offset == -2, 1.0, value)
    return value


def kernel(
    n, hs, kh, nx,
    slots, d_hbm, a_hbm, out_ref,
    gbuf, pbuf, abuf, apbuf, ebuf, epbuf,
    d_st, dx_st, dr_st, f_st, fx_st, fr_st, a_st, ax_st, ar_st, e_st, ex_st, er_st,
    run, run_e, sbuf, sbuf_e, xbuf, xbuf_e, tbuf, tbuf_e, rbuf, rbuf_e, radial, axial, slots_e,
    local_d, local_a,
    right_send, right_recv, left_send, left_recv,
    core_send, core_recv, adj_send, adj_recv,
    edge_send, edge_recv, edge_core_send, edge_core_recv, slots_sem,
    slab_send, slab_recv, slab_send_e, slab_recv_e,
    cross_send, cross_recv, cross_send_e, cross_recv_e,
):
    me = lax.axis_index("mode")
    my_harm = lax.axis_index("harm")
    core = lax.axis_index("rad")
    per_owner = n // hs
    cells = nx // n
    wide = d_hbm.shape[0]
    chunk = axial.shape[0]
    first, last = me == 0, me == n - 1
    low_helper, high_helper = me == 1, me == n - 2

    for k in range(FIELDS):
        pltpu.make_async_copy(d_hbm.at[:, ORDER[k]], gbuf.at[me, k], local_d.at[k]).start()
    for k in range(FIELDS):
        pltpu.make_async_copy(a_hbm.at[:, ORDER[k]], abuf.at[k], local_a.at[k]).start()

    barrier = pltpu.get_barrier_semaphore()

    def greet(index, carry):
        q = index // hs
        h = index % hs

        @pl.when(jnp.logical_or(q != me, h != my_harm))
        def _():
            pl.semaphore_signal(barrier, inc=1, device_id={"mode": q, "harm": h}, device_id_type=MESH)

        return carry

    lax.fori_loop(0, n * hs, greet, 0)
    pl.semaphore_signal(barrier, inc=1, device_id={"rad": 1 - core}, device_id_type=MESH)

    row = lax.broadcasted_iota(jnp.int32, (128, 128), 0)
    col = lax.broadcasted_iota(jnp.int32, (128, 128), 1)
    shift = (1 - 2 * core) * 128
    radial[0:128, :] = coefficient(row - col).astype(jnp.bfloat16)
    radial[128:256, :] = coefficient(row - col + shift).astype(jnp.bfloat16)
    row = lax.broadcasted_iota(jnp.int32, (chunk, chunk), 0)
    col = lax.broadcasted_iota(jnp.int32, (chunk, chunk), 1)
    same = (row // nx) == (col // nx)
    axial[...] = jnp.where(same, coefficient(col - row), 0.0).astype(jnp.bfloat16)
    run[...] = jnp.zeros_like(run)
    run_e[...] = jnp.zeros_like(run_e)

    pl.semaphore_wait(barrier, n * hs)

    def remote(src, dst, send, recv, target):
        return pltpu.make_async_remote_copy(
            src_ref=src, dst_ref=dst, send_sem=send, recv_sem=recv,
            device_id=target, device_id_type=MESH)

    other = {"rad": 1 - core}

    def to_right(block, k):
        return remote(gbuf.at[block, k], gbuf.at[block, k],
                      right_send.at[block, k], right_recv.at[block, k], {"mode": me + 1})

    def to_left(block, k):
        return remote(gbuf.at[block, k], gbuf.at[block, k],
                      left_send.at[block, k], left_recv.at[block, k], {"mode": me - 1})

    def to_core(block, k):
        return remote(gbuf.at[block, k], pbuf.at[block, k],
                      core_send.at[block, k], core_recv.at[block, k], other)

    def adjoint_to_core(k):
        return remote(abuf.at[k], apbuf.at[k], adj_send.at[k], adj_recv.at[k], other)

    def edge(k, target):
        return remote(abuf.at[k], ebuf.at[k], edge_send.at[k], edge_recv.at[k], {"mode": target})

    def edge_to_core(k):
        return remote(ebuf.at[k], epbuf.at[k], edge_core_send.at[k], edge_core_recv.at[k], other)

    def edge_slots(target):
        return remote(slots, slots_e, slots_sem.at[0], slots_sem.at[1], {"mode": target})

    for k in range(FIELDS):
        pltpu.make_async_copy(d_hbm.at[:, ORDER[k]], gbuf.at[me, k], local_d.at[k]).wait()

        @pl.when(me < n - 1)
        def _():
            to_right(me, k).start()

        @pl.when(me > 0)
        def _():
            to_left(me, k).start()

        to_core(me, k).start()

    for k in range(FIELDS):
        pltpu.make_async_copy(a_hbm.at[:, ORDER[k]], abuf.at[k], local_a.at[k]).wait()
        adjoint_to_core(k).start()

    @pl.when(first)
    def _():
        edge_slots(1).start()

    @pl.when(last)
    def _():
        edge_slots(n - 2).start()

    def prepare(own, partner, plain, along_x, along_r, k):
        group = chunk // nx

        def step(i, carry):
            at = pl.ds(i * group, group)
            to = pl.ds(k * wide + i * group, group)
            mine = own[at].reshape(chunk, 128)
            both = jnp.concatenate([mine, partner[at].reshape(chunk, 128)], axis=1)
            shape = (group, nx, 128)

            @pl.when(k < 2)
            def _():
                plain[to] = mine.astype(jnp.float32).reshape(shape)

            along_r[to] = jnp.dot(
                both, radial[...], preferred_element_type=jnp.float32).reshape(shape)
            along_x[to] = jnp.dot(
                axial[...], mine, preferred_element_type=jnp.float32).reshape(shape)
            return carry

        lax.fori_loop(0, wide // group, step, 0)

    def products(table, stop, total, dirs, adjs, k):
        d_pl, d_x, d_r = dirs
        a_pl, a_x, a_r = adjs

        def one_mode(m, carry):
            da = table[m, 0, stop] * 2
            dd = table[m, 1, stop] * 2
            for half in range(nx // 8):
                part = pl.ds(half * 8, 8)
                real = total[(k * SLOTS + m) * 2, part, :]
                imag = total[(k * SLOTS + m) * 2 + 1, part, :]
                for c in range(kh):
                    ia = c * SLOTS * 2 + da
                    id_ = c * SLOTS * 2 + dd
                    d1r = d_pl[id_, part, :]
                    d1i = d_pl[id_ + 1, part, :]
                    d2r = d_pl[wide + id_, part, :]
                    d2i = d_pl[wide + id_ + 1, part, :]
                    a1r = a_pl[ia, part, :]
                    a1i = a_pl[ia + 1, part, :]
                    a2r = a_pl[wide + ia, part, :]
                    a2i = a_pl[wide + ia + 1, part, :]
                    axr = a_x[k * wide + ia, part, :]
                    axi = a_x[k * wide + ia + 1, part, :]
                    arr = a_r[k * wide + ia, part, :]
                    ari = a_r[k * wide + ia + 1, part, :]
                    dxr = d_x[k * wide + id_, part, :]
                    dxi = d_x[k * wide + id_ + 1, part, :]
                    drr = d_r[k * wide + id_, part, :]
                    dri = d_r[k * wide + id_ + 1, part, :]
                    real = real + (
                        ((d1r * axr + d1i * axi) + (d2r * arr + d2i * ari))
                        + ((dxr * a1r + dxi * a1i) + (drr * a2r + dri * a2i)))
                    imag = imag + (
                        ((d1r * axi - d1i * axr) + (d2r * ari - d2i * arr))
                        + ((dxr * a1i - dxi * a1r) + (drr * a2i - dri * a2r)))
                total[(k * SLOTS + m) * 2, part, :] = real
                total[(k * SLOTS + m) * 2 + 1, part, :] = imag
            return carry

        lax.fori_loop(0, SLOTS, one_mode, 0)

    def ready(k, act):
        def step(c, carry):
            act(c)
            return carry

        low = jnp.where(k == 0, 1, jnp.where(k == 1, 0, k))
        lax.fori_loop(low, k + 1, step, 0)

    left_side = (d_st, dx_st, dr_st)
    right_side = (f_st, fx_st, fr_st)
    own_adjoint = (a_st, ax_st, ar_st)
    edge_adjoint = (e_st, ex_st, er_st)

    def visit(block, stop, k, side):
        to_core(block, k).wait_recv()
        prepare(gbuf.at[block, k], pbuf.at[block, k], *side, k)
        ready(k, lambda c: products(slots, stop, run, side, own_adjoint, c))

    def visit_edge(stop, k, side):
        edge_to_core(k).wait_recv()
        prepare(ebuf.at[k], epbuf.at[k], *edge_adjoint, k)
        ready(k, lambda c: products(slots_e, stop, run_e, side, edge_adjoint, c))

    def arrive_chunk(hop, k):
        from_left = me - hop
        from_right = me + hop

        @pl.when(from_left >= 0)
        def _():
            to_right(from_left, k).wait_recv()

            @pl.when(jnp.logical_and(me < n - 1, jnp.logical_or(me < n - 2, from_left > 0)))
            def _():
                to_right(from_left, k).start()

            to_core(from_left, k).start()

        @pl.when(from_right < n)
        def _():
            to_left(from_right, k).wait_recv()

            @pl.when(jnp.logical_and(me > 0, jnp.logical_or(me > 1, from_right < n - 1)))
            def _():
                to_left(from_right, k).start()

            to_core(from_right, k).start()

        @pl.when(jnp.logical_and(hop == 1, first))
        def _():
            to_right(me, k).wait_send()
            edge(k, 1).start()

        @pl.when(jnp.logical_and(hop == 1, last))
        def _():
            to_left(me, k).wait_send()
            edge(k, n - 2).start()

        @pl.when(jnp.logical_and(hop == n - 2, jnp.logical_or(low_helper, high_helper)))
        def _():
            edge(k, me).wait_recv()
            edge_to_core(k).start()

    def visit_chunk(hop, k):
        @pl.when(me - hop >= 0)
        def _():
            visit(me - hop, hop, k, left_side)

            @pl.when(jnp.logical_and(hop == n - 2, high_helper))
            def _():
                visit_edge(n - 1, k, left_side)

        @pl.when(me + hop < n)
        def _():
            visit(me + hop, n - hop, k, right_side)

            @pl.when(jnp.logical_and(hop == n - 2, low_helper))
            def _():
                visit_edge(1, k, right_side)

    scale = 1.0 / (12.0 * math.sqrt(8.0 * n * HARMS))
    owner = me // per_owner
    place = me % per_owner
    helper = jnp.logical_or(low_helper, high_helper)
    side = jnp.where(low_helper, 0, 1)
    owner_e = jnp.where(low_helper, 0, hs - 1)

    piece = SLOTS * 2 // hs

    def slab(k, q, h, i):
        return remote(tbuf.at[k, q], rbuf.at[k, i, pl.ds(h * piece, piece)],
                      slab_send.at[k, q], slab_recv.at[k, h * per_owner + i],
                      {"mode": q, "harm": owner})

    def slab_e(k, q, h, i):
        return remote(tbuf_e.at[k, q], rbuf_e.at[k, i, pl.ds(h * piece, piece)],
                      slab_send_e.at[k, q], slab_recv_e.at[k, i * hs + h],
                      {"mode": q, "harm": owner_e})

    def each_target(k, act):
        def step(q, carry):
            @pl.when(jnp.logical_or(q != me, owner != my_harm))
            def _():
                act(slab(k, q, my_harm, place))

            @pl.when(jnp.logical_and(helper, jnp.logical_or(q != me, owner_e != my_harm)))
            def _():
                act(slab_e(k, q, my_harm, side))

            return carry

        lax.fori_loop(0, n, step, 0)

    def cross(k, target, sender):
        return remote(sbuf.at[k, :, pl.ds(target * piece, piece)], xbuf.at[k, sender],
                      cross_send.at[k, target], cross_recv.at[k, sender], {"harm": target})

    def cross_e(k, target, sender):
        return remote(sbuf_e.at[k, :, pl.ds(target * piece, piece)], xbuf_e.at[k, sender],
                      cross_send_e.at[k, target], cross_recv_e.at[k, sender], {"harm": target})

    def each_partner(act):
        def step(h, carry):
            @pl.when(h != my_harm)
            def _():
                act(h)

            return carry

        lax.fori_loop(0, hs, step, 0)

    own_piece = pl.ds(my_harm * piece, piece)

    def share(k):
        span = pl.ds(k * SLOTS * 2, SLOTS * 2)
        for q in range(n):
            sbuf[k, q] = run[span, q * cells:(q + 1) * cells, :] * scale
        each_partner(lambda h: cross(k, h, my_harm).start())
        xbuf[k, my_harm] = sbuf[k, :, own_piece]

        @pl.when(helper)
        def _():
            for q in range(n):
                sbuf_e[k, q] = run_e[span, q * cells:(q + 1) * cells, :] * scale
            each_partner(lambda h: cross_e(k, h, my_harm).start())
            xbuf_e[k, my_harm] = sbuf_e[k, :, own_piece]

    def deliver(k):
        each_partner(lambda h: cross(k, h, h).wait_recv())
        total = xbuf[k, 0]
        for h in range(1, hs):
            total = total + xbuf[k, h]
        tbuf[k] = total

        @pl.when(helper)
        def _():
            each_partner(lambda h: cross_e(k, h, h).wait_recv())
            total = xbuf_e[k, 0]
            for h in range(1, hs):
                total = total + xbuf_e[k, h]
            tbuf_e[k] = total

        each_target(k, lambda copy: copy.start())

        @pl.when(owner == my_harm)
        def _():
            rbuf[k, place, own_piece] = tbuf[k, me]

        @pl.when(jnp.logical_and(helper, owner_e == my_harm))
        def _():
            rbuf_e[k, side, own_piece] = tbuf_e[k, me]

    def own_chunk(k, carry):
        adjoint_to_core(k).wait_recv()
        prepare(abuf.at[k], apbuf.at[k], *own_adjoint, k)
        visit(me, 0, k, left_side)
        return carry

    lax.fori_loop(0, FIELDS, own_chunk, 0)

    @pl.when(jnp.logical_or(low_helper, high_helper))
    def _():
        edge_slots(me).wait_recv()

    count = (n - 2) * FIELDS

    def steps(i, carry):
        @pl.when(i < count)
        def _():
            arrive_chunk(1 + i // FIELDS, i % FIELDS)

        @pl.when(i > 0)
        def _():
            visit_chunk(1 + (i - 1) // FIELDS, (i - 1) % FIELDS)

        @pl.when(i > count - FIELDS)
        def _():
            ready(i - 1 - (count - FIELDS), share)

        @pl.when(i > count - FIELDS + 1)
        def _():
            ready(i - 2 - (count - FIELDS), deliver)

        return carry

    lax.fori_loop(0, count + 1, steps, 0)
    deliver(FIELDS - 1)

    def collect(k, carry):
        def arrive(index, inner):
            h = index // per_owner
            i = index % per_owner
            mine = jnp.logical_and(h == my_harm, my_harm * per_owner + i == me)

            @pl.when(jnp.logical_not(mine))
            def _():
                slab(k, 0, h, i).wait_recv()

            return inner

        lax.fori_loop(0, hs * per_owner, arrive, 0)
        field = jnp.where(k < 2, k + 1, jnp.where(k == 2, 0, k))
        for i in range(per_owner):
            out_ref[i, :, field] = rbuf[k, i]

        for i, source, holder, spot in ((0, 1, 0, 0), (1, n - 2, hs - 1, per_owner - 1)):
            @pl.when(my_harm == holder)
            def _(i=i, source=source, spot=spot):
                def wait_edge(h, inner):
                    @pl.when(jnp.logical_or(h != my_harm, me != source))
                    def _():
                        slab_e(k, 0, h, i).wait_recv()

                    return inner

                lax.fori_loop(0, hs, wait_edge, 0)
                out_ref[spot, :, field] = out_ref[spot, :, field] + rbuf_e[k, i]

        return carry

    lax.fori_loop(0, FIELDS, collect, 0)

    def drain_slabs(k, carry):
        each_target(k, lambda copy: copy.wait_send())
        each_partner(lambda h: cross(k, h, my_harm).wait_send())

        @pl.when(helper)
        def _():
            each_partner(lambda h: cross_e(k, h, my_harm).wait_send())

        return carry

    lax.fori_loop(0, FIELDS, drain_slabs, 0)

    def drain(i, carry):
        block = i // FIELDS
        k = i % FIELDS

        @pl.when(jnp.logical_not(jnp.logical_or(
            jnp.logical_and(first, block == n - 1), jnp.logical_and(last, block == 0))))
        def _():
            to_core(block, k).wait_send()

        @pl.when(jnp.logical_and(
            jnp.logical_and(block <= me, me < n - 1),
            jnp.logical_and(
                jnp.logical_or(me < n - 2, block > 0),
                jnp.logical_not(first))))
        def _():
            to_right(block, k).wait_send()

        @pl.when(jnp.logical_and(
            jnp.logical_and(block >= me, me > 0),
            jnp.logical_and(
                jnp.logical_or(me > 1, block < n - 1),
                jnp.logical_not(last))))
        def _():
            to_left(block, k).wait_send()

        return carry

    lax.fori_loop(0, n * FIELDS, drain, 0)

    def drain_adjoint(k, carry):
        adjoint_to_core(k).wait_send()

        @pl.when(jnp.logical_or(first, last))
        def _():
            edge(k, me).wait_send()

        @pl.when(helper)
        def _():
            edge_to_core(k).wait_send()

        return carry

    lax.fori_loop(0, FIELDS, drain_adjoint, 0)

    @pl.when(jnp.logical_or(first, last))
    def _():
        edge_slots(me).wait_send()


def body(hs, direct_field, adjoint_field, triad_slots):
    n = triad_slots.shape[1]
    kh = direct_field.shape[0]
    nx = direct_field.shape[4]
    wide = kh * SLOTS * 2
    chunk = min(256, wide * nx)
    cells = nx // n
    per_owner = n // hs
    f32, bf16 = jnp.float32, jnp.bfloat16
    dma = pltpu.SemaphoreType.DMA
    slab_shape = (SLOTS * 2, cells, 128)
    piece = SLOTS * 2 // hs
    block = (FIELDS, wide, nx, 128)
    stage = [
        pltpu.VMEM((2 * wide, nx, 128), f32),
        pltpu.VMEM((FIELDS * wide, nx, 128), f32),
        pltpu.VMEM((FIELDS * wide, nx, 128), f32),
    ]
    c = FIELDS
    out = pl.pallas_call(
        functools.partial(kernel, n, hs, kh, nx),
        out_shape=jax.ShapeDtypeStruct((per_owner, SLOTS * 2, FIELDS, cells, 128), f32),
        in_specs=[pl.BlockSpec(memory_space=pltpu.SMEM)] + [pl.BlockSpec(memory_space=pltpu.HBM)] * 2,
        out_specs=pl.BlockSpec(memory_space=pltpu.VMEM),
        scratch_shapes=[pltpu.VMEM((n,) + block, bf16)] * 2
        + [pltpu.VMEM(block, bf16)] * 4
        + stage * 4
        + [pltpu.VMEM((FIELDS * SLOTS * 2, nx, 128), f32)] * 2
        + [
            pltpu.VMEM((c, n) + slab_shape, f32),
            pltpu.VMEM((c, n) + slab_shape, f32),
            pltpu.VMEM((c, hs, n, piece) + slab_shape[1:], f32),
            pltpu.VMEM((c, hs, n, piece) + slab_shape[1:], f32),
            pltpu.VMEM((c, n, piece) + slab_shape[1:], f32),
            pltpu.VMEM((c, n, piece) + slab_shape[1:], f32),
            pltpu.VMEM((c, per_owner) + slab_shape, f32),
            pltpu.VMEM((c, 2) + slab_shape, f32),
            pltpu.VMEM((256, 128), bf16),
            pltpu.VMEM((chunk, chunk), bf16),
            pltpu.SMEM((SLOTS, 2, n), jnp.int32),
            dma((c,)), dma((c,)),
            dma((n, c)), dma((n, c)), dma((n, c)), dma((n, c)),
            dma((n, c)), dma((n, c)), dma((c,)), dma((c,)),
            dma((c,)), dma((c,)), dma((c,)), dma((c,)), dma((2,)),
            dma((c, n)), dma((c, hs * per_owner)), dma((c, n)), dma((c, 2 * hs)),
            dma((c, hs)), dma((c, hs)), dma((c, hs)), dma((c, hs)),
        ],
        compiler_params=pltpu.CompilerParams(
            collective_id=0, has_side_effects=True, vmem_limit_bytes=56_000_000),
    )(
        jnp.transpose(triad_slots, (0, 2, 1)),
        direct_field.reshape(wide, FIELDS, nx, 128),
        adjoint_field.reshape(wide, FIELDS, nx, 128),
    )
    return out.reshape(per_owner * SLOTS, 2, FIELDS, cells, 128)


def solution(mesh):
    return jax.shard_map(
        functools.partial(body, mesh.shape["harm"]),
        mesh=mesh,
        in_specs=(
            P(("case", "harm"), "mode", None, None, None, "rad"),
            P(("case", "harm"), "mode", None, None, None, "rad"),
            P("mode", None, None),
        ),
        out_specs=P(("case", "harm"), None, None, "mode", "rad"),
        check_vma=False,
    )
```

```python
import functools
import math

import jax
import jax.numpy as jnp
from jax import lax
from jax.experimental import pallas as pl
from jax.experimental.pallas import tpu as pltpu
from jax.sharding import PartitionSpec as P

HARMS = 8
SLOTS = 4
FIELDS = 5
ORDER = (1, 2, 0, 3, 4)
MESH = pl.DeviceIdType.MESH


def coefficient(offset):
    value = jnp.where(offset == 1, 8.0, 0.0)
    value = jnp.where(offset == -1, -8.0, value)
    value = jnp.where(offset == 2, -1.0, value)
    value = jnp.where(offset == -2, 1.0, value)
    return value


def kernel(
    n, hs, kh, nx,
    slots, d_hbm, a_hbm, out_ref,
    gbuf, pbuf, abuf, apbuf, ebuf, epbuf,
    d_st, dx_st, dr_st, f_st, fx_st, fr_st, a_st, ax_st, ar_st, e_st, ex_st, er_st,
    run, run_e, sbuf, sbuf_e, rbuf, rbuf_e, radial, axial, slots_e,
    local_d, local_a,
    right_send, right_recv, left_send, left_recv,
    core_send, core_recv, adj_send, adj_recv,
    edge_send, edge_recv, edge_core_send, edge_core_recv, slots_sem,
    slab_send, slab_recv, slab_send_e, slab_recv_e,
):
    me = lax.axis_index("mode")
    my_harm = lax.axis_index("harm")
    core = lax.axis_index("rad")
    per_owner = n // hs
    cells = nx // n
    wide = d_hbm.shape[0]
    chunk = axial.shape[0]
    first, last = me == 0, me == n - 1
    low_helper, high_helper = me == 1, me == n - 2

    for k in range(FIELDS):
        pltpu.make_async_copy(d_hbm.at[:, ORDER[k]], gbuf.at[me, k], local_d.at[k]).start()
    for k in range(FIELDS):
        pltpu.make_async_copy(a_hbm.at[:, ORDER[k]], abuf.at[k], local_a.at[k]).start()

    barrier = pltpu.get_barrier_semaphore()

    def greet(index, carry):
        q = index // hs
        h = index % hs

        @pl.when(jnp.logical_or(q != me, h != my_harm))
        def _():
            pl.semaphore_signal(barrier, inc=1, device_id={"mode": q, "harm": h}, device_id_type=MESH)

        return carry

    lax.fori_loop(0, n * hs, greet, 0)
    pl.semaphore_signal(barrier, inc=1, device_id={"rad": 1 - core}, device_id_type=MESH)

    row = lax.broadcasted_iota(jnp.int32, (128, 128), 0)
    col = lax.broadcasted_iota(jnp.int32, (128, 128), 1)
    shift = (1 - 2 * core) * 128
    radial[0:128, :] = coefficient(row - col).astype(jnp.bfloat16)
    radial[128:256, :] = coefficient(row - col + shift).astype(jnp.bfloat16)
    row = lax.broadcasted_iota(jnp.int32, (chunk, chunk), 0)
    col = lax.broadcasted_iota(jnp.int32, (chunk, chunk), 1)
    same = (row // nx) == (col // nx)
    axial[...] = jnp.where(same, coefficient(col - row), 0.0).astype(jnp.bfloat16)
    run[...] = jnp.zeros_like(run)
    run_e[...] = jnp.zeros_like(run_e)

    pl.semaphore_wait(barrier, n * hs)

    def remote(src, dst, send, recv, target):
        return pltpu.make_async_remote_copy(
            src_ref=src, dst_ref=dst, send_sem=send, recv_sem=recv,
            device_id=target, device_id_type=MESH)

    other = {"rad": 1 - core}

    def to_right(block, k):
        return remote(gbuf.at[block, k], gbuf.at[block, k],
                      right_send.at[block, k], right_recv.at[block, k], {"mode": me + 1})

    def to_left(block, k):
        return remote(gbuf.at[block, k], gbuf.at[block, k],
                      left_send.at[block, k], left_recv.at[block, k], {"mode": me - 1})

    def to_core(block, k):
        return remote(gbuf.at[block, k], pbuf.at[block, k],
                      core_send.at[block, k], core_recv.at[block, k], other)

    def adjoint_to_core(k):
        return remote(abuf.at[k], apbuf.at[k], adj_send.at[k], adj_recv.at[k], other)

    def edge(k, target):
        return remote(abuf.at[k], ebuf.at[k], edge_send.at[k], edge_recv.at[k], {"mode": target})

    def edge_to_core(k):
        return remote(ebuf.at[k], epbuf.at[k], edge_core_send.at[k], edge_core_recv.at[k], other)

    def edge_slots(target):
        return remote(slots, slots_e, slots_sem.at[0], slots_sem.at[1], {"mode": target})

    for k in range(FIELDS):
        pltpu.make_async_copy(d_hbm.at[:, ORDER[k]], gbuf.at[me, k], local_d.at[k]).wait()

        @pl.when(me < n - 1)
        def _():
            to_right(me, k).start()

        @pl.when(me > 0)
        def _():
            to_left(me, k).start()

        to_core(me, k).start()

    for k in range(FIELDS):
        pltpu.make_async_copy(a_hbm.at[:, ORDER[k]], abuf.at[k], local_a.at[k]).wait()
        adjoint_to_core(k).start()

    @pl.when(first)
    def _():
        edge_slots(1).start()

    @pl.when(last)
    def _():
        edge_slots(n - 2).start()

    def prepare(own, partner, plain, along_x, along_r, k):
        group = chunk // nx

        def step(i, carry):
            at = pl.ds(i * group, group)
            to = pl.ds(k * wide + i * group, group)
            mine = own[at].reshape(chunk, 128)
            both = jnp.concatenate([mine, partner[at].reshape(chunk, 128)], axis=1)
            shape = (group, nx, 128)

            @pl.when(k < 2)
            def _():
                plain[to] = mine.astype(jnp.float32).reshape(shape)

            along_r[to] = jnp.dot(
                both, radial[...], preferred_element_type=jnp.float32).reshape(shape)
            along_x[to] = jnp.dot(
                axial[...], mine, preferred_element_type=jnp.float32).reshape(shape)
            return carry

        lax.fori_loop(0, wide // group, step, 0, unroll=True)

    def products(table, stop, total, dirs, adjs, k):
        d_pl, d_x, d_r = dirs
        a_pl, a_x, a_r = adjs

        def one_mode(m, carry):
            da = table[m, 0, stop] * 2
            dd = table[m, 1, stop] * 2
            for half in range(nx // 8):
                part = pl.ds(half * 8, 8)
                real = total[(k * SLOTS + m) * 2, part, :]
                imag = total[(k * SLOTS + m) * 2 + 1, part, :]
                for c in range(kh):
                    ia = c * SLOTS * 2 + da
                    id_ = c * SLOTS * 2 + dd
                    d1r = d_pl[id_, part, :]
                    d1i = d_pl[id_ + 1, part, :]
                    d2r = d_pl[wide + id_, part, :]
                    d2i = d_pl[wide + id_ + 1, part, :]
                    a1r = a_pl[ia, part, :]
                    a1i = a_pl[ia + 1, part, :]
                    a2r = a_pl[wide + ia, part, :]
                    a2i = a_pl[wide + ia + 1, part, :]
                    axr = a_x[k * wide + ia, part, :]
                    axi = a_x[k * wide + ia + 1, part, :]
                    arr = a_r[k * wide + ia, part, :]
                    ari = a_r[k * wide + ia + 1, part, :]
                    dxr = d_x[k * wide + id_, part, :]
                    dxi = d_x[k * wide + id_ + 1, part, :]
                    drr = d_r[k * wide + id_, part, :]
                    dri = d_r[k * wide + id_ + 1, part, :]
                    real = real + (
                        ((d1r * axr + d1i * axi) + (d2r * arr + d2i * ari))
                        + ((dxr * a1r + dxi * a1i) + (drr * a2r + dri * a2i)))
                    imag = imag + (
                        ((d1r * axi - d1i * axr) + (d2r * ari - d2i * arr))
                        + ((dxr * a1i - dxi * a1r) + (drr * a2i - dri * a2r)))
                total[(k * SLOTS + m) * 2, part, :] = real
                total[(k * SLOTS + m) * 2 + 1, part, :] = imag
            return carry

        lax.fori_loop(0, SLOTS, one_mode, 0)

    def ready(k, act):
        def step(c, carry):
            act(c)
            return carry

        low = jnp.where(k == 0, 1, jnp.where(k == 1, 0, k))
        lax.fori_loop(low, k + 1, step, 0)

    left_side = (d_st, dx_st, dr_st)
    right_side = (f_st, fx_st, fr_st)
    own_adjoint = (a_st, ax_st, ar_st)
    edge_adjoint = (e_st, ex_st, er_st)

    def visit(block, stop, k, side):
        to_core(block, k).wait_recv()
        prepare(gbuf.at[block, k], pbuf.at[block, k], *side, k)
        ready(k, lambda c: products(slots, stop, run, side, own_adjoint, c))

    def visit_edge(stop, k, side):
        edge_to_core(k).wait_recv()
        prepare(ebuf.at[k], epbuf.at[k], *edge_adjoint, k)
        ready(k, lambda c: products(slots_e, stop, run_e, side, edge_adjoint, c))

    def arrive_chunk(hop, k):
        from_left = me - hop
        from_right = me + hop

        @pl.when(from_left >= 0)
        def _():
            to_right(from_left, k).wait_recv()

            @pl.when(jnp.logical_and(me < n - 1, jnp.logical_or(me < n - 2, from_left > 0)))
            def _():
                to_right(from_left, k).start()

            to_core(from_left, k).start()

        @pl.when(from_right < n)
        def _():
            to_left(from_right, k).wait_recv()

            @pl.when(jnp.logical_and(me > 0, jnp.logical_or(me > 1, from_right < n - 1)))
            def _():
                to_left(from_right, k).start()

            to_core(from_right, k).start()

        @pl.when(jnp.logical_and(hop == 1, first))
        def _():
            to_right(me, k).wait_send()
            edge(k, 1).start()

        @pl.when(jnp.logical_and(hop == 1, last))
        def _():
            to_left(me, k).wait_send()
            edge(k, n - 2).start()

        @pl.when(jnp.logical_and(hop == n - 2, jnp.logical_or(low_helper, high_helper)))
        def _():
            edge(k, me).wait_recv()
            edge_to_core(k).start()

    def visit_chunk(hop, k):
        @pl.when(me - hop >= 0)
        def _():
            visit(me - hop, hop, k, left_side)

            @pl.when(jnp.logical_and(hop == n - 2, high_helper))
            def _():
                visit_edge(n - 1, k, left_side)

        @pl.when(me + hop < n)
        def _():
            visit(me + hop, n - hop, k, right_side)

            @pl.when(jnp.logical_and(hop == n - 2, low_helper))
            def _():
                visit_edge(1, k, right_side)

    scale = 1.0 / (12.0 * math.sqrt(8.0 * n * HARMS))
    owner = me // per_owner
    place = me % per_owner
    helper = jnp.logical_or(low_helper, high_helper)
    side = jnp.where(low_helper, 0, 1)
    owner_e = jnp.where(low_helper, 0, hs - 1)

    def slab(k, q, h, i):
        return remote(sbuf.at[k, q], rbuf.at[k, h * per_owner + i],
                      slab_send.at[k, q], slab_recv.at[k, h * per_owner + i],
                      {"mode": q, "harm": owner})

    def slab_e(k, q, h, i):
        return remote(sbuf_e.at[k, q], rbuf_e.at[k, i * hs + h],
                      slab_send_e.at[k, q], slab_recv_e.at[k, i * hs + h],
                      {"mode": q, "harm": owner_e})

    def each_target(k, act):
        def step(index, carry):
            q = jnp.where(me < n // 2, n - 1 - index, index)

            @pl.when(jnp.logical_or(q != me, owner != my_harm))
            def _():
                act(slab(k, q, my_harm, place))

            @pl.when(jnp.logical_and(helper, jnp.logical_or(q != me, owner_e != my_harm)))
            def _():
                act(slab_e(k, q, my_harm, side))

            return carry

        lax.fori_loop(0, n, step, 0)

    def deliver(k):
        span = pl.ds(k * SLOTS * 2, SLOTS * 2)
        for q in range(n):
            sbuf[k, q] = run[span, q * cells:(q + 1) * cells, :] * scale

        @pl.when(helper)
        def _():
            for q in range(n):
                sbuf_e[k, q] = run_e[span, q * cells:(q + 1) * cells, :] * scale

        each_target(k, lambda copy: copy.start())

        @pl.when(owner == my_harm)
        def _():
            rbuf[k, my_harm * per_owner + place] = sbuf[k, me]

        @pl.when(jnp.logical_and(helper, owner_e == my_harm))
        def _():
            rbuf_e[k, side * hs + my_harm] = sbuf_e[k, me]

    def own_chunk(k, carry):
        adjoint_to_core(k).wait_recv()
        prepare(abuf.at[k], apbuf.at[k], *own_adjoint, k)
        visit(me, 0, k, left_side)
        return carry

    lax.fori_loop(0, FIELDS, own_chunk, 0)

    @pl.when(jnp.logical_or(low_helper, high_helper))
    def _():
        edge_slots(me).wait_recv()

    count = (n - 2) * FIELDS

    def steps(i, carry):
        @pl.when(i < count)
        def _():
            arrive_chunk(1 + i // FIELDS, i % FIELDS)

        @pl.when(i > 0)
        def _():
            visit_chunk(1 + (i - 1) // FIELDS, (i - 1) % FIELDS)

        @pl.when(i > count - FIELDS)
        def _():
            ready(i - 1 - (count - FIELDS), deliver)

        return carry

    lax.fori_loop(0, count + 1, steps, 0)

    def collect(k, carry):
        def arrive(index, inner):
            h = index // per_owner
            i = index % per_owner
            mine = jnp.logical_and(h == my_harm, my_harm * per_owner + i == me)

            @pl.when(jnp.logical_not(mine))
            def _():
                slab(k, 0, h, i).wait_recv()

            return inner

        lax.fori_loop(0, hs * per_owner, arrive, 0)
        field = jnp.where(k < 2, k + 1, jnp.where(k == 2, 0, k))
        for i in range(per_owner):
            total = rbuf[k, i]
            for h in range(1, hs):
                total = total + rbuf[k, h * per_owner + i]
            out_ref[i, :, field] = total

        for i, source, holder, spot in ((0, 1, 0, 0), (1, n - 2, hs - 1, per_owner - 1)):
            @pl.when(my_harm == holder)
            def _(i=i, source=source, spot=spot):
                def wait_edge(h, inner):
                    @pl.when(jnp.logical_or(h != my_harm, me != source))
                    def _():
                        slab_e(k, 0, h, i).wait_recv()

                    return inner

                lax.fori_loop(0, hs, wait_edge, 0)
                total = out_ref[spot, :, field]
                for h in range(hs):
                    total = total + rbuf_e[k, i * hs + h]
                out_ref[spot, :, field] = total

        return carry

    lax.fori_loop(0, FIELDS, collect, 0)

    def drain_slabs(k, carry):
        each_target(k, lambda copy: copy.wait_send())
        return carry

    lax.fori_loop(0, FIELDS, drain_slabs, 0)

    def drain(i, carry):
        block = i // FIELDS
        k = i % FIELDS

        @pl.when(jnp.logical_not(jnp.logical_or(
            jnp.logical_and(first, block == n - 1), jnp.logical_and(last, block == 0))))
        def _():
            to_core(block, k).wait_send()

        @pl.when(jnp.logical_and(
            jnp.logical_and(block <= me, me < n - 1),
            jnp.logical_and(
                jnp.logical_or(me < n - 2, block > 0),
                jnp.logical_not(first))))
        def _():
            to_right(block, k).wait_send()

        @pl.when(jnp.logical_and(
            jnp.logical_and(block >= me, me > 0),
            jnp.logical_and(
                jnp.logical_or(me > 1, block < n - 1),
                jnp.logical_not(last))))
        def _():
            to_left(block, k).wait_send()

        return carry

    lax.fori_loop(0, n * FIELDS, drain, 0)

    def drain_adjoint(k, carry):
        adjoint_to_core(k).wait_send()

        @pl.when(jnp.logical_or(first, last))
        def _():
            edge(k, me).wait_send()

        @pl.when(helper)
        def _():
            edge_to_core(k).wait_send()

        return carry

    lax.fori_loop(0, FIELDS, drain_adjoint, 0)

    @pl.when(jnp.logical_or(first, last))
    def _():
        edge_slots(me).wait_send()


def body(hs, direct_field, adjoint_field, triad_slots):
    n = triad_slots.shape[1]
    kh = direct_field.shape[0]
    nx = direct_field.shape[4]
    wide = kh * SLOTS * 2
    chunk = min(256, wide * nx)
    cells = nx // n
    per_owner = n // hs
    f32, bf16 = jnp.float32, jnp.bfloat16
    dma = pltpu.SemaphoreType.DMA
    slab_shape = (SLOTS * 2, cells, 128)
    block = (FIELDS, wide, nx, 128)
    stage = [
        pltpu.VMEM((2 * wide, nx, 128), f32),
        pltpu.VMEM((FIELDS * wide, nx, 128), f32),
        pltpu.VMEM((FIELDS * wide, nx, 128), f32),
    ]
    c = FIELDS
    out = pl.pallas_call(
        functools.partial(kernel, n, hs, kh, nx),
        out_shape=jax.ShapeDtypeStruct((per_owner, SLOTS * 2, FIELDS, cells, 128), f32),
        in_specs=[pl.BlockSpec(memory_space=pltpu.SMEM)] + [pl.BlockSpec(memory_space=pltpu.HBM)] * 2,
        out_specs=pl.BlockSpec(memory_space=pltpu.VMEM),
        scratch_shapes=[pltpu.VMEM((n,) + block, bf16)] * 2
        + [pltpu.VMEM(block, bf16)] * 4
        + stage * 4
        + [pltpu.VMEM((FIELDS * SLOTS * 2, nx, 128), f32)] * 2
        + [
            pltpu.VMEM((c, n) + slab_shape, f32),
            pltpu.VMEM((c, n) + slab_shape, f32),
            pltpu.VMEM((c, hs * per_owner) + slab_shape, f32),
            pltpu.VMEM((c, 2 * hs) + slab_shape, f32),
            pltpu.VMEM((256, 128), bf16),
            pltpu.VMEM((chunk, chunk), bf16),
            pltpu.SMEM((SLOTS, 2, n), jnp.int32),
            dma((c,)), dma((c,)),
            dma((n, c)), dma((n, c)), dma((n, c)), dma((n, c)),
            dma((n, c)), dma((n, c)), dma((c,)), dma((c,)),
            dma((c,)), dma((c,)), dma((c,)), dma((c,)), dma((2,)),
            dma((c, n)), dma((c, hs * per_owner)), dma((c, n)), dma((c, 2 * hs)),
        ],
        compiler_params=pltpu.CompilerParams(
            collective_id=0, has_side_effects=True, vmem_limit_bytes=56_000_000),
    )(
        jnp.transpose(triad_slots, (0, 2, 1)),
        direct_field.reshape(wide, FIELDS, nx, 128),
        adjoint_field.reshape(wide, FIELDS, nx, 128),
    )
    return out.reshape(per_owner * SLOTS, 2, FIELDS, cells, 128)


def solution(mesh):
    return jax.shard_map(
        functools.partial(body, mesh.shape["harm"]),
        mesh=mesh,
        in_specs=(
            P(("case", "harm"), "mode", None, None, None, "rad"),
            P(("case", "harm"), "mode", None, None, None, "rad"),
            P("mode", None, None),
        ),
        out_specs=P(("case", "harm"), None, None, "mode", "rad"),
        check_vma=False,
    )
```
